128 devices in a mesh: gx: 16 (over x, z), gz: 8 (over y, core).
Axes of the slice: x: 4, y: 4, z: 4, core: 2. Of those that a mesh axis runs over, the one named last changes fastest.
Arguments:
- grains: float32 [8, 128, 128, 256], P(None, 'gx', 'gz'), may hold values from 0 to 1
- block_owner: int32 [32, 32, 64], P('gx', 'gz'), may hold values from 0 to 127, as said below
- element_anchor: int32 [65536], P(('gx', 'gz')), may hold values from 0 to 1023, as said below
- strain_step: float32 [6, 8, 65536], P(None, None, ('gx', 'gz')), may hold values from -3 to 3
- stress: float32 [6, 8, 65536], P(None, None, ('gx', 'gz')), may hold values from -6 to 6
- resistance: float32 [24, 8, 65536], P(None, None, ('gx', 'gz')), may hold values from 0.5 to 2
- slip_active: int32 [24, 65536], P(None, ('gx', 'gz')), may hold values 0 or 1
- orientation_schmid: float32 [8, 24, 6], replicated, may hold values from -2.5 to 2.5
- latent_hardening: float32 [24, 24], replicated, may hold values from 0.2 to 1.4
- mobility: float32 [8], replicated, may hold values from 0.5 to 2
- grain_state: float32 [8], replicated, may hold values from 0 to 1
Outputs:
- grains_out: float32 [8, 128, 128, 256], P(None, 'gx', 'gz')
- stress_out: float32 [6, 8, 65536], P(None, None, ('gx', 'gz'))
- resistance_out: float32 [24, 8, 65536], P(None, None, ('gx', 'gz'))
The draws below stay inside these ranges and needn't reach their ends.
Inputs may be any that keep to these rules, and one draw needn't show every extreme that they name: `block_owner`: the 512 blocks of one device name any one owner at most 8 times, and some owner exactly 8 times; every device owns exactly 512 blocks. `element_anchor`: element d * 512 + l holds the block that home s sends to owner d as its r-th one (rank as in the reference program), written s * 8 + r; every block belongs to exactly one element.
All inputs are finite; a program needn't handle non-finite values. No bound on the sum of `slip_active` on one device may be relied on, other than what follows from the above.
Results may differ from the reference program's by a relative error of at most 0.0003.
Values sent between devices are 32-bit elements; how exact they have to be, the bound alone decides.
No kernel may reach another device: no remote copies, remote signals or barrier semaphores. Data moves between devices by JAX's collectives and lax.ppermute only.
A program may use at most 64 MiB of HBM per device.

```python
import math
import jax
import jax.numpy as jnp
from jax import lax

P_SIZE = 8
NS = 24
NQ = 8
ITERS = 4
STEPS = 3
SUB = 2
CX = 8
CZ = 16
NY = 256
NX = 128
NZ = 128
BLK_DEV = 512
ELEMS = 65536
CAP = 8
N_GX = 16
N_GZ = 8


def pair_rank_drawn(owners, count_all):
    onehot = (owners[:, None] == jnp.arange(count_all, dtype=jnp.int32)[None, :]).astype(jnp.int32)
    before = jnp.cumsum(onehot, axis=0) - onehot
    return jnp.sum(before * onehot, axis=1).astype(jnp.int32)


def routing_tables(key):
    count_all = N_GX * N_GZ
    per_dev = BLK_DEV
    base_load = per_dev // count_all
    capacity = 2 * base_load
    base_key = jax.random.fold_in(key, 911)
    key_offsets = jax.random.fold_in(base_key, 1)
    key_shifts = jax.random.fold_in(base_key, 2)
    key_orders = jax.random.fold_in(base_key, 3)
    key_slots = jax.random.fold_in(base_key, 4)
    offset_order = jax.random.permutation(key_offsets, count_all).astype(jnp.int32)
    shifts = jax.random.randint(key_shifts, (count_all // 2,), 0, base_load + 1).astype(jnp.int32).at[0].set(base_load)
    load = jnp.full((count_all,), base_load, jnp.int32).at[offset_order[0::2]].add(shifts).at[offset_order[1::2]].add(-shifts)
    seg_end = jnp.cumsum(load)
    sequence = jnp.arange(per_dev, dtype=jnp.int32)
    offset_of = jnp.sum((sequence[:, None] >= seg_end[None, :]).astype(jnp.int32), axis=1)
    sources = jnp.arange(count_all, dtype=jnp.int32)
    orderings = jax.vmap(lambda src: jax.random.permutation(jax.random.fold_in(key_orders, src), per_dev))(sources).astype(jnp.int32)
    dest_seq = (sources[:, None] + offset_of[None, :]) % count_all
    owners = jnp.zeros((count_all, per_dev), jnp.int32).at[sources[:, None], orderings].set(dest_seq)
    ranks = lax.map(lambda row: pair_rank_drawn(row, count_all), owners)
    counts = load[(sources[None, :] - sources[:, None]) % count_all]
    starts = jnp.cumsum(counts, axis=0) - counts
    arrival = starts[sources[:, None], owners] + ranks
    shuffles = jax.vmap(lambda dst: jax.random.permutation(jax.random.fold_in(key_slots, dst), per_dev))(sources).astype(jnp.int32)
    slots = shuffles[owners, arrival]
    anchor = jnp.zeros((count_all, per_dev), jnp.int32).at[owners, slots].set(sources[:, None] * capacity + ranks)
    return (owners, anchor)


def draw_block_owner(key, part):
    owners, anchor = routing_tables(key)
    shaped = owners.reshape(N_GX, N_GZ, CX // 4, CZ // 4, NY // 4).transpose(0, 2, 1, 3, 4)
    return shaped.reshape(N_GX * (CX // 4), N_GZ * (CZ // 4), NY // 4)


def draw_element_anchor(key, part):
    owners, anchor = routing_tables(key)
    return anchor.reshape(-1)


def plant(result, own_key, smallest, top_value):
    longest = result.shape.index(max(result.shape))
    spots = []
    for shift in (0, 1):
        where = [jax.random.randint(jax.random.fold_in(own_key, axis), (), 0, length) for axis, length in enumerate(result.shape)]
        where[longest] = (where[longest] + shift) % result.shape[longest]
        spots.append(tuple(where))
    return result.at[spots[0]].set(smallest).at[spots[1]].set(top_value)


def block_levels(rng, extent, cuts, low, high):
    gain, own = 1.0, jax.random.fold_in(rng, 6)
    for dim, parts in cuts:
        steps = jnp.exp(jax.random.uniform(jax.random.fold_in(own, dim), (parts,), jnp.float32, low / len(cuts), high / len(cuts)))
        gain = gain * jnp.repeat(steps, extent[dim] // parts).reshape([-1 if axis == dim else 1 for axis in range(len(extent))])
    return gain


def centred(rng, dims, scale, reach, shards=(), kind=jnp.bfloat16):
    values = jax.random.normal(rng, dims, jnp.float32) * scale
    if len(shards) > 0:
        values = block_levels(rng, dims, shards, -0.22, 0.18) * values
    return jnp.clip(values, min=-reach, max=reach).astype(kind)


def setup_inputs(seed: int = 0) -> dict:
    key_of = jax.random.split(jax.random.key(seed), 12)
    grains = jnp.clip(1.0 * jax.random.uniform(key_of[0], (P_SIZE, NX, NZ, NY), jnp.float32) ** block_levels(key_of[0], (P_SIZE, NX, NZ, NY), ((1, 16), (2, 8)), -0.2, 0.2), 0.0, 1.0)
    block_owner = draw_block_owner(jax.random.fold_in(key_of[11], 71), 0)
    element_anchor = draw_element_anchor(jax.random.fold_in(key_of[11], 71), 0)
    strain_step = centred(key_of[3], (6, NQ, ELEMS), 0.5, 3.0, ((2, 128),), jnp.float32)
    stress = centred(key_of[4], (6, NQ, ELEMS), 1.0, 6.0, ((2, 128),), jnp.float32)
    resistance = jnp.clip(jnp.exp(math.log(2.0) - 1.3862944 * jax.random.uniform(key_of[5], (NS, NQ, ELEMS), jnp.float32) ** block_levels(key_of[5], (NS, NQ, ELEMS), ((2, 128),), -0.2, 0.2)), 0.5, 2.0)
    slip_active = plant((jax.random.randint(key_of[6], (NS, ELEMS), 0, 4) < 3).astype(jnp.int32), jax.random.fold_in(key_of[6], 1), 0, 1)
    orientation_schmid = centred(key_of[7], (P_SIZE, NS, 6), 6 ** -0.5, 2.5, (), jnp.float32)
    latent_hardening = jnp.clip(jax.random.uniform(key_of[8], (NS, NS), jnp.float32, 0.2, 1.4), 0.2, 1.4)
    mobility = jnp.clip(jnp.exp(jax.random.uniform(key_of[9], (P_SIZE,), jnp.float32, math.log(0.5), math.log(2.0))), 0.5, 2.0)
    grain_state = jnp.clip(jax.random.uniform(key_of[10], (P_SIZE,), jnp.float32, 0.0, 1.0), 0.0, 1.0)
    return {"grains": grains, "block_owner": block_owner, "element_anchor": element_anchor, "strain_step": strain_step, "stress": stress, "resistance": resistance, "slip_active": slip_active, "orientation_schmid": orientation_schmid, "latent_hardening": latent_hardening, "mobility": mobility, "grain_state": grain_state}


CROSS_TERM = 1.5
DRIVE_SCALE = 6.0
TIME_STEP = 0.02
SLIP_RATE = 0.1
HARDENING = 0.5
HIGHEST = lax.Precision.HIGHEST


def column_map(width):
    quarter = width // 4
    row_index = jnp.arange(width, dtype=jnp.int32)[:, None]
    col_index = jnp.arange(2 * quarter, dtype=jnp.int32)[None, :]
    member = ((row_index // 4) == (col_index % quarter)) & (((row_index % 4) // 2) == (col_index // quarter))
    return member.astype(jnp.float32)


def restrict(field):
    orders, size_x, size_z, size_y = field.shape
    squares = (field * field).reshape(orders * size_x * size_z, size_y)
    along_y = jnp.dot(squares, column_map(size_y), precision=HIGHEST, preferred_element_type=jnp.float32)
    along_y = along_y.reshape(orders, size_x // 4, 2, 2, size_z // 4, 2, 2, 2, size_y // 4)
    averaged = jnp.sum(along_y, axis=(3, 6)) * 0.125
    averaged = averaged.transpose(0, 2, 4, 5, 1, 3, 6)
    return averaged.reshape(orders * 8, (size_x // 4) * (size_z // 4) * (size_y // 4))


def prolong(stored, size_x, size_z, size_y):
    quarter = size_y // 4
    spread = stored.reshape(2, 2, 2, size_x // 4, size_z // 4, quarter).transpose(3, 0, 4, 1, 2, 5)
    spread = spread.reshape((size_x // 4) * 2 * (size_z // 4) * 2, 2 * quarter)
    cell_energy = jnp.dot(spread, column_map(size_y).T, precision=HIGHEST, preferred_element_type=jnp.float32)
    cell_energy = cell_energy.reshape(size_x // 4, 2, 1, size_z // 4, 2, 1, size_y)
    cell_energy = jnp.broadcast_to(cell_energy, (size_x // 4, 2, 2, size_z // 4, 2, 2, size_y))
    return cell_energy.reshape(size_x, size_z, size_y)


def pair_rank(owners, count_all):
    onehot = (owners[:, None] == jnp.arange(count_all, dtype=jnp.int32)[None, :]).astype(jnp.int32)
    before = jnp.cumsum(onehot, axis=0) - onehot
    return jnp.sum(before * onehot, axis=1).astype(jnp.int32)


def mechanics(mix_weights, strain_step, stress, resistance, slip_active, orientation_schmid, latent_hardening):
    orders, systems = orientation_schmid.shape[0], orientation_schmid.shape[1]
    points, elements = stress.shape[1], stress.shape[2]
    flat = points * elements
    weights_flat = mix_weights.reshape(orders, flat)
    tensor = jnp.dot(orientation_schmid.reshape(orders, systems * 6).T, weights_flat, precision=HIGHEST, preferred_element_type=jnp.float32).reshape(systems, 6, flat)
    trial_stress = (stress + 2.0 * strain_step).reshape(6, flat)
    active = jnp.broadcast_to(slip_active.astype(jnp.float32)[:, None, :], (systems, points, elements)).reshape(systems, flat)
    resist = resistance.reshape(systems, flat)
    stress_now = trial_stress
    slip_amount = jnp.zeros((systems, flat), jnp.float32)
    for sweep in range(ITERS):
        resolved = jnp.sum(tensor * stress_now[None, :, :], axis=1)
        slip_amount = active * SLIP_RATE * resolved / (resist + jnp.abs(resolved))
        stress_now = trial_stress - 2.0 * jnp.sum(tensor * slip_amount[:, None, :], axis=0)
    harden = jnp.dot(latent_hardening, jnp.abs(slip_amount), precision=HIGHEST, preferred_element_type=jnp.float32)
    resist_new = resist + HARDENING * harden
    stored = jnp.sum(resist_new * jnp.abs(slip_amount), axis=0)
    return stress_now.reshape(6, points, elements), resist_new.reshape(systems, points, elements), stored.reshape(points, elements)


def phase_update(center, x_plus, x_minus, z_plus, z_minus, energy, mobility, grain_state):
    laplace = x_plus + x_minus + z_plus + z_minus + jnp.roll(center, 1, 3) + jnp.roll(center, -1, 3) - 6.0 * center
    sum_squares = jnp.sum(center * center, axis=0, keepdims=True)
    keep_share = (1.0 - grain_state)[:, None, None, None]
    driving = -center + center * center * center + 2.0 * CROSS_TERM * center * (sum_squares - center * center) - laplace + 2.0 * DRIVE_SCALE * energy[None] * keep_share * center
    return center - TIME_STEP * mobility[:, None, None, None] * driving


def reference(grains, block_owner, element_anchor, strain_step, stress, resistance, slip_active, orientation_schmid, latent_hardening, mobility, grain_state):
    count_all = N_GX * N_GZ
    per_dev = BLK_DEV
    capacity = CAP
    size_x, size_z, size_y = grains.shape[1], grains.shape[2], grains.shape[3]
    owners = block_owner.reshape(N_GX, CX // 4, N_GZ, CZ // 4, NY // 4).transpose(0, 2, 1, 3, 4).reshape(count_all, per_dev)
    ranks = lax.map(lambda row: pair_rank(row, count_all), owners)
    sources = jnp.arange(count_all, dtype=jnp.int32)[:, None]
    mailbox = (owners * count_all + sources) * capacity + ranks
    block_table = jnp.zeros((count_all * count_all * capacity,), jnp.int32).at[mailbox.reshape(-1)].set(jnp.arange(count_all * per_dev, dtype=jnp.int32))
    wanted = (sources * (count_all * capacity) + element_anchor.reshape(count_all, per_dev)).reshape(-1)
    element_block = block_table[wanted]

    def to_groups(array):
        return jnp.moveaxis(array.reshape(array.shape[:-1] + (count_all, per_dev)), -2, 0)

    def from_groups(array):
        return jnp.moveaxis(array, 0, -2).reshape(array.shape[1:-1] + (count_all * per_dev,))

    def one_group(pieces):
        return mechanics(pieces[0], pieces[1], pieces[2], pieces[3], pieces[4], orientation_schmid, latent_hardening)

    points = stress.shape[1]
    for cycle in range(STEPS):
        weights = restrict(grains)
        feature = weights.shape[0]
        by_source = weights.reshape(feature, N_GX, CX // 4, N_GZ, CZ // 4, NY // 4).transpose(0, 1, 3, 2, 4, 5).reshape(feature, count_all * per_dev)
        elem_weights = by_source[:, element_block].reshape(feature // points, points, count_all * per_dev)
        new_stress, new_resist, stored = lax.map(one_group, (to_groups(elem_weights), to_groups(strain_step), to_groups(stress), to_groups(resistance), to_groups(slip_active)))
        stress = from_groups(new_stress)
        resistance = from_groups(new_resist)
        stored_all = from_groups(stored)
        stored_source = jnp.zeros_like(stored_all).at[:, element_block].set(stored_all)
        stored_grid = stored_source.reshape(points, N_GX, N_GZ, CX // 4, CZ // 4, NY // 4).transpose(0, 1, 3, 2, 4, 5).reshape(points, -1)
        cell_energy = prolong(stored_grid, size_x, size_z, size_y)
        for inner in range(SUB):
            grains = phase_update(grains, jnp.roll(grains, -1, 1), jnp.roll(grains, 1, 1), jnp.roll(grains, -1, 2), jnp.roll(grains, 1, 2), cell_energy, mobility, grain_state)
    return grains, stress, resistance
```

```python
import jax
import jax.numpy as jnp
from jax import lax
from jax.sharding import PartitionSpec as P

ITERS = 4
STEPS = 3
SUB = 2


CROSS_TERM = 1.5
DRIVE_SCALE = 6.0
TIME_STEP = 0.02
SLIP_RATE = 0.1
HARDENING = 0.5
HIGHEST = lax.Precision.HIGHEST


def in_blocks(array, dim, size):
    lengths = array.shape
    parts = array.reshape(*lengths[:dim], size, lengths[dim] // size, *lengths[dim + 1 :])
    return jnp.moveaxis(parts, dim, 0)


def joined_along(parts, dim):
    parts = jnp.moveaxis(parts, 0, dim)
    lengths = parts.shape
    return parts.reshape(*lengths[:dim], lengths[dim] * lengths[dim + 1], *lengths[dim + 2 :])


def exchange_both(array, axis, axes, splits, concats):
    sizes = [lax.axis_size(a) for a in axes]
    parts = in_blocks(array, splits[0], sizes[0])
    parts = jnp.moveaxis(in_blocks(parts, splits[1] + 1, sizes[1]), 0, 1)
    inside = parts.shape[2:]
    parts = parts.reshape(-1, *inside)
    parts = lax.all_to_all(parts, axis, split_axis=0, concat_axis=0, tiled=True)
    parts = joined_along(parts.reshape(*sizes, *inside), concats[0] + 1)
    return joined_along(parts, concats[1])


def padded_2(array, sides, width):
    for axis, dim in sides:
        size, length = (lax.axis_size(axis), array.shape[dim])
        up = [(i, (i + 1) % size) for i in range(size)]
        down = [(j, i) for i, j in up]
        last = lax.slice_in_dim(array, length - width, length, axis=dim)
        first = lax.slice_in_dim(array, 0, width, axis=dim)
        before = lax.ppermute(last, axis, up)
        after = lax.ppermute(first, axis, down)
        array = jnp.concatenate([before, array, after], axis=dim)
    return array


def column_map(width):
    quarter = width // 4
    row_index = jnp.arange(width, dtype=jnp.int32)[:, None]
    col_index = jnp.arange(2 * quarter, dtype=jnp.int32)[None, :]
    member = (row_index // 4 == col_index % quarter) & (row_index % 4 // 2 == col_index // quarter)
    return member.astype(jnp.float32)


def restrict(field):
    orders, size_x, size_z, size_y = field.shape
    squares = (field * field).reshape(orders * size_x * size_z, size_y)
    along_y = jnp.dot(
        squares, column_map(size_y), precision=HIGHEST, preferred_element_type=jnp.float32
    )
    along_y = along_y.reshape(orders, size_x // 4, 2, 2, size_z // 4, 2, 2, 2, size_y // 4)
    averaged = jnp.sum(along_y, axis=(3, 6)) * 0.125
    averaged = averaged.transpose(0, 2, 4, 5, 1, 3, 6)
    return averaged.reshape(orders * 8, size_x // 4 * (size_z // 4) * (size_y // 4))


def prolong(stored, size_x, size_z, size_y):
    quarter = size_y // 4
    spread = stored.reshape(2, 2, 2, size_x // 4, size_z // 4, quarter).transpose(3, 0, 4, 1, 2, 5)
    spread = spread.reshape(size_x // 4 * 2 * (size_z // 4) * 2, 2 * quarter)
    cell_energy = jnp.dot(
        spread, column_map(size_y).T, precision=HIGHEST, preferred_element_type=jnp.float32
    )
    cell_energy = cell_energy.reshape(size_x // 4, 2, 1, size_z // 4, 2, 1, size_y)
    cell_energy = jnp.broadcast_to(cell_energy, (size_x // 4, 2, 2, size_z // 4, 2, 2, size_y))
    return cell_energy.reshape(size_x, size_z, size_y)


def pair_rank(owners, count_all):
    onehot = (owners[:, None] == jnp.arange(count_all, dtype=jnp.int32)[None, :]).astype(jnp.int32)
    before = jnp.cumsum(onehot, axis=0) - onehot
    return jnp.sum(before * onehot, axis=1)


def mechanics(
    mix_weights, strain_step, stress, resistance, slip_active, orientation_schmid, latent_hardening
):
    orders, systems = (orientation_schmid.shape[0], orientation_schmid.shape[1])
    points, elements = (stress.shape[1], stress.shape[2])
    flat = points * elements
    weights_flat = mix_weights.reshape(orders, flat)
    schmid_rows = orientation_schmid.transpose(2, 1, 0).reshape(6 * systems, orders)
    tensor = jnp.dot(
        schmid_rows, weights_flat, precision=HIGHEST, preferred_element_type=jnp.float32
    ).reshape(6, systems, flat)
    trial_stress = (stress + 2.0 * strain_step).reshape(6, flat)
    active = jnp.broadcast_to(
        slip_active.astype(jnp.float32)[:, None, :], (systems, points, elements)
    ).reshape(systems, flat)
    resist = resistance.reshape(systems, flat)
    components = [trial_stress[comp] for comp in range(6)]
    slip_amount = jnp.zeros((systems, flat), jnp.float32)
    for sweep in range(ITERS):
        resolved = tensor[0] * components[0][None, :]
        for comp in range(1, 6):
            resolved = resolved + tensor[comp] * components[comp][None, :]
        slip_amount = active * SLIP_RATE * resolved / (resist + jnp.abs(resolved))
        components = [
            trial_stress[comp] - 2.0 * jnp.sum(tensor[comp] * slip_amount, axis=0)
            for comp in range(6)
        ]
    stress_now = jnp.stack(components, axis=0)
    harden = jnp.dot(
        latent_hardening,
        jnp.abs(slip_amount),
        precision=HIGHEST,
        preferred_element_type=jnp.float32,
    )
    resist_new = resist + HARDENING * harden
    stored = jnp.sum(resist_new * jnp.abs(slip_amount), axis=0)
    return (
        stress_now.reshape(6, points, elements),
        resist_new.reshape(systems, points, elements),
        stored.reshape(points, elements),
    )


def phase_update(center, x_plus, x_minus, z_plus, z_minus, energy, mobility, grain_state):
    laplace = (
        x_plus
        + x_minus
        + z_plus
        + z_minus
        + jnp.roll(center, 1, 3)
        + jnp.roll(center, -1, 3)
        - 6.0 * center
    )
    sum_squares = jnp.sum(center * center, axis=0, keepdims=True)
    keep_share = (1.0 - grain_state)[:, None, None, None]
    driving = (
        -center
        + center * center * center
        + 2.0 * CROSS_TERM * center * (sum_squares - center * center)
        - laplace
        + 2.0 * DRIVE_SCALE * energy[None] * keep_share * center
    )
    return center - TIME_STEP * mobility[:, None, None, None] * driving


def advance(padded, energy, mobility, grain_state):
    center = padded[:, 1:-1, 1:-1]
    return phase_update(
        center,
        padded[:, 2:, 1:-1],
        padded[:, :-2, 1:-1],
        padded[:, 1:-1, 2:],
        padded[:, 1:-1, :-2],
        energy,
        mobility,
        grain_state,
    )


def neighbours(array, axis, dim, width):
    size, length = (lax.axis_size(axis), array.shape[dim])
    up = [(i, (i + 1) % size) for i in range(size)]
    down = [(j, i) for i, j in up]
    last = lax.slice_in_dim(array, length - width, length, axis=dim)
    first = lax.slice_in_dim(array, 0, width, axis=dim)
    return lax.ppermute(last, axis, up), lax.ppermute(first, axis, down)


def routed(packed, slots):
    count = lax.axis_size(("gx", "gz"))
    feature = packed.shape[-1]
    sent = packed.reshape(count, slots // count, feature)
    got = lax.all_to_all(sent, ("gx", "gz"), split_axis=0, concat_axis=0, tiled=True)
    return got.reshape(slots, feature)


def shards(
    grains,
    block_owner,
    element_anchor,
    strain_step,
    stress,
    resistance,
    slip_active,
    orientation_schmid,
    latent_hardening,
    mobility,
    grain_state,
):
    count_all = lax.axis_size(("gx", "gz"))
    owners = block_owner.reshape(-1)
    per_dev = owners.shape[0]
    capacity = 2 * per_dev // count_all
    slots_all = count_all * capacity
    mailbox = owners * capacity + pair_rank(owners, count_all)
    slot_index = jnp.arange(slots_all, dtype=jnp.int32)
    slot_hit = (slot_index[:, None] == mailbox[None, :]).astype(jnp.float32)
    element_pick = (element_anchor[:, None] == slot_index[None, :]).astype(jnp.float32)
    orders, size_x, size_z, size_y = grains.shape
    points = stress.shape[1]
    systems = resistance.shape[0]
    state = jnp.concatenate(
        [
            strain_step.reshape(6 * points, per_dev),
            stress.reshape(6 * points, per_dev),
            resistance.reshape(systems * points, per_dev),
            slip_active.astype(jnp.float32),
        ],
        axis=0,
    )
    width = state.shape[0]
    state = jnp.pad(state, ((0, -width % 128), (0, 0)))
    outbox = lax.dot_general(
        element_pick,
        state,
        (((0,), (1,)), ((), ())),
        precision=HIGHEST,
        preferred_element_type=jnp.float32,
    )
    inbox = routed(outbox, slots_all)
    home = lax.dot_general(
        inbox,
        slot_hit,
        (((0,), (0,)), ((), ())),
        precision=HIGHEST,
        preferred_element_type=jnp.float32,
    )
    strain_h = home[: 6 * points].reshape(6, points, per_dev)
    stress_h = home[6 * points : 12 * points].reshape(6, points, per_dev)
    resist_h = home[12 * points : 12 * points + systems * points].reshape(
        systems, points, per_dev
    )
    active_h = home[12 * points + systems * points : width]
    for cycle in range(STEPS):
        weights = restrict(grains).reshape(orders, points, per_dev)
        padded = padded_2(grains, (("gx", 1), ("gz", 2)), SUB)
        stress_h, resist_h, stored = mechanics(
            weights, strain_h, stress_h, resist_h, active_h, orientation_schmid, latent_hardening
        )
        cell_energy = prolong(stored, size_x, size_z, size_y)
        x_lo, x_hi = neighbours(cell_energy, "gx", 0, 1)
        z_lo, z_hi = neighbours(cell_energy, "gz", 1, 1)
        side = [jnp.pad(e, ((1, 1), (0, 0), (0, 0))) for e in (z_lo, z_hi)]
        energy_pad = jnp.concatenate([x_lo, cell_energy, x_hi], axis=0)
        energy_pad = jnp.concatenate([side[0], energy_pad, side[1]], axis=1)
        field = advance(padded, energy_pad, mobility, grain_state)
        grains = advance(field, cell_energy, mobility, grain_state)
    back = jnp.concatenate(
        [stress_h.reshape(6 * points, per_dev), resist_h.reshape(systems * points, per_dev)],
        axis=0,
    )
    width = back.shape[0]
    back = jnp.pad(back, ((0, -width % 128), (0, 0)))
    outbox = lax.dot_general(
        slot_hit,
        back,
        (((1,), (1,)), ((), ())),
        precision=HIGHEST,
        preferred_element_type=jnp.float32,
    )
    inbox = routed(outbox, slots_all)
    owned = lax.dot_general(
        inbox,
        element_pick,
        (((0,), (1,)), ((), ())),
        precision=HIGHEST,
        preferred_element_type=jnp.float32,
    )
    stress = owned[: 6 * points].reshape(6, points, per_dev)
    resistance = owned[6 * points : width].reshape(systems, points, per_dev)
    return (grains, stress, resistance)


def solution(mesh):
    return jax.shard_map(
        shards,
        mesh=mesh,
        in_specs=(
            P(None, "gx", "gz", None),
            P("gx", "gz", None),
            P(("gx", "gz")),
            P(None, None, ("gx", "gz")),
            P(None, None, ("gx", "gz")),
            P(None, None, ("gx", "gz")),
            P(None, ("gx", "gz")),
            P(),
            P(),
            P(),
            P(),
        ),
        out_specs=(
            P(None, "gx", "gz", None),
            P(None, None, ("gx", "gz")),
            P(None, None, ("gx", "gz")),
        ),
        check_vma=False,
    )
```

```python
import functools

import jax
import jax.numpy as jnp
from jax import lax
from jax.experimental import pallas as pl
from jax.experimental.pallas import tpu as pltpu
from jax.sharding import PartitionSpec as P

ITERS = 4
STEPS = 3
SUB = 2

CROSS_TERM = 1.5
DRIVE_SCALE = 6.0
TIME_STEP = 0.02
SLIP_RATE = 0.1
HARDENING = 0.5
LANES = 128
BF16 = jnp.bfloat16
F32 = jnp.float32
VMEM_BYTES = 24 << 20


def two_terms(value):
    high = value.astype(BF16)
    low = (value - high.astype(F32)).astype(BF16)
    return high, low


def two_terms_outside(value):
    high = lax.reduce_precision(value, 8, 7)
    low = lax.reduce_precision(value - high, 8, 7)
    return high.astype(BF16), low.astype(BF16)


def product(left, right):
    return lax.dot_general(
        left, right, (((1,), (0,)), ((), ())), preferred_element_type=F32
    )


def product_rows(left, right):
    return lax.dot_general(
        left, right, (((1,), (1,)), ((), ())), preferred_element_type=F32
    )


def call(kernel, shapes, scratch=(), **options):
    return pl.pallas_call(
        kernel,
        out_shape=shapes,
        scratch_shapes=list(scratch),
        compiler_params=pltpu.CompilerParams(vmem_limit_bytes=VMEM_BYTES),
        **options,
    )


def shape(*dims):
    return jax.ShapeDtypeStruct(dims, F32)


def into_slots(slots_row, values, slots_all):
    items = values.shape[1]
    slot = lax.broadcasted_iota(jnp.int32, (slots_all, items), 0)
    hit = (slot == slots_row).astype(F32).astype(BF16)
    high, low = two_terms(values)
    return product_rows(hit, high) + product_rows(hit, low)


def out_of_slots(slots_col, mail):
    items = slots_col.shape[0]
    slots_all = mail.shape[0]
    lane = lax.broadcasted_iota(jnp.int32, (items, LANES), 1)
    hit = jnp.concatenate(
        [
            (lane + start == slots_col).astype(F32).astype(BF16)
            for start in range(0, slots_all, LANES)
        ],
        axis=1,
    )
    high, low = two_terms(mail)
    return jnp.transpose(product(hit, high) + product(hit, low))


def pack_state_kernel(anchor, strain, stress, resist, active, out):
    rows = strain.shape[0] + stress.shape[0] + resist.shape[0] + active.shape[0]
    values = jnp.concatenate(
        [
            strain[...],
            stress[...],
            resist[...],
            active[...].astype(F32),
            jnp.zeros((out.shape[1] - rows, strain.shape[1]), F32),
        ],
        axis=0,
    )
    out[...] = into_slots(anchor[...], values, out.shape[0])


def unpack_state_kernel(mailbox, mail, strain, stress, resist, active):
    values = out_of_slots(mailbox[...], mail[...])
    start = 0
    for part in (strain, stress, resist, active):
        part[...] = values[start : start + part.shape[0]]
        start += part.shape[0]


def pack_result_kernel(mailbox, stress, resist, out):
    rows = stress.shape[0] + resist.shape[0]
    values = jnp.concatenate(
        [
            stress[...],
            resist[...],
            jnp.zeros((out.shape[1] - rows, stress.shape[1]), F32),
        ],
        axis=0,
    )
    out[...] = into_slots(mailbox[...], values, out.shape[0])


def unpack_result_kernel(anchor, mail, stress, resist):
    values = out_of_slots(anchor[...], mail[...])
    stress[...] = values[: stress.shape[0]]
    resist[...] = values[stress.shape[0] : stress.shape[0] + resist.shape[0]]


def routed(packed):
    count = lax.axis_size(("gx", "gz"))
    slots, feature = packed.shape
    sent = packed.reshape(count, slots // count, feature)
    got = lax.all_to_all(sent, ("gx", "gz"), split_axis=0, concat_axis=0, tiled=True)
    return got.reshape(slots, feature)


def bits(index, *sizes):
    found = []
    for size in reversed(sizes):
        found.append(index % size)
        index = index // size
    return list(reversed(found))


def row_map():
    to_half, to_i, to_bx, to_pair, to_qx, to_qz, _ = bits(
        jnp.arange(128, dtype=jnp.int32)[:, None], 2, 2, 2, 2, 2, 2, 2
    )
    i, bx, qx, pair, half, qz, _ = bits(
        jnp.arange(128, dtype=jnp.int32)[None, :], 2, 2, 2, 2, 2, 2, 2
    )
    same = (
        (to_half == half)
        & (to_i == i)
        & (to_bx == bx)
        & (to_pair == pair)
        & (to_qx == qx)
        & (to_qz == qz)
    )
    half_map = jnp.where(same, 0.125, 0.0)
    return jnp.concatenate([half_map, half_map], axis=1).astype(BF16)


def lane_map(size_y):
    by, qy, _ = bits(jnp.arange(size_y, dtype=jnp.int32)[:, None], size_y // 4, 2, 2)
    to_qy, to_half, to_by = bits(
        jnp.arange(size_y, dtype=jnp.int32)[None, :], 2, 2, size_y // 4
    )
    found = (by == to_by) & (qy == to_qy)
    maps = [jnp.where(found & (to_half == half), 1.0, 0.0) for half in range(2)]
    return jnp.concatenate(maps + maps, axis=0).astype(BF16)


def spread_map(size_y):
    by, qy, _ = bits(jnp.arange(size_y, dtype=jnp.int32)[None, :], size_y // 4, 2, 2)
    of_qy, _, of_by = bits(jnp.arange(size_y, dtype=jnp.int32)[:, None], 2, 2, size_y // 4)
    found = jnp.where((by == of_by) & (qy == of_qy), 1.0, 0.0)
    return jnp.concatenate([found, found], axis=0).astype(BF16)


def repeat_map():
    to_qy, to_qx, _, to_qz, _ = bits(
        jnp.arange(32, dtype=jnp.int32)[:, None], 2, 2, 2, 2, 2
    )
    qx, qz, qy = bits(jnp.arange(8, dtype=jnp.int32)[None, :], 2, 2, 2)
    found = jnp.where((to_qy == qy) & (to_qx == qx) & (to_qz == qz), 1.0, 0.0)
    return jnp.concatenate([found, found], axis=1).astype(BF16)


def restrict_kernel(grains, rows, lanes, weights):
    orders, size_x, size_z, size_y = grains.shape
    lefts = []
    for pair in range(orders // 2):
        parts = []
        for order in (2 * pair, 2 * pair + 1):
            for coarse in range(size_x // 2):
                low = grains[order, 2 * coarse]
                high = grains[order, 2 * coarse + 1]
                parts.append(low * low + high * high)
        summed = jnp.concatenate(parts, axis=0)
        moved = product(rows[...], jnp.concatenate(two_terms(summed), axis=0))
        high, low = two_terms(moved)
        lefts.append(
            jnp.concatenate([high[:64], high[64:], low[:64], low[64:]], axis=1)
        )
    found = product(jnp.concatenate(lefts, axis=0), lanes[...])
    row = lax.broadcasted_iota(jnp.int32, (found.shape[0], LANES), 0)
    picked = jnp.where(row % 2 == 0, found[:, :LANES], found[:, LANES:])
    for order in range(orders):
        for tile in range(4):
            start = (order * 4 + tile) * 8
            weights[order * 8 : order * 8 + 8, tile * LANES : (tile + 1) * LANES] = picked[
                start : start + 8
            ]


def prolonged(stored, repeat, spread, energy):
    high, low = two_terms(stored)
    rows = product(repeat, jnp.concatenate([high, low], axis=0))
    row = lax.broadcasted_iota(jnp.int32, rows.shape, 0)
    lane = lax.broadcasted_iota(jnp.int32, rows.shape, 1)
    rows = jnp.where((row // 4) % 2 == (lane // 64) % 2, rows, 0.0)
    tiles = [
        jnp.concatenate(
            [rows[:16, t * LANES : (t + 1) * LANES], rows[16:, t * LANES : (t + 1) * LANES]],
            axis=1,
        )
        for t in range(4)
    ]
    left = jnp.concatenate(two_terms(jnp.concatenate(tiles, axis=0)), axis=1)
    cells = product(left, spread)
    for bx in range(2):
        for pair in range(2):
            for qx in range(2):
                start = ((bx * 2 + pair) * 2 + qx) * 8
                energy[bx * 2 + qx, pair * 8 : pair * 8 + 8] = cells[start : start + 8]


def mechanics_kernel(
    weights,
    strain,
    stress,
    resist,
    active,
    tensor_map,
    harden_map,
    active_map,
    repeat,
    spread,
    stress_out,
    resist_out,
    energy,
    tensor,
    rates,
    amounts,
):
    systems = active.shape[0]
    points = resist.shape[0] // systems
    items = weights.shape[1]
    high, low = two_terms(weights[...])
    tensor[...] = product(tensor_map[...], jnp.concatenate([high, low, high], axis=0))
    rates[...] = product(active_map[...], active[...].astype(BF16)) * SLIP_RATE

    def tile_step(tile, carry):
        lanes = pl.ds(pl.multiple_of(tile * LANES, LANES), LANES)
        trial = [
            stress[points * c : points * (c + 1), lanes]
            + 2.0 * strain[points * c : points * (c + 1), lanes]
            for c in range(6)
        ]

        def sweep(_, now):
            sums = [jnp.zeros((points, LANES), F32) for _ in range(6)]
            for a in range(systems):
                rows = pl.ds(a * points, points)
                parts = [tensor[pl.ds((a * 6 + c) * points, points), lanes] for c in range(6)]
                resolved = (
                    (parts[0] * now[0] + parts[1] * now[1])
                    + (parts[2] * now[2] + parts[3] * now[3])
                    + (parts[4] * now[4] + parts[5] * now[5])
                )
                slip = rates[rows, lanes] * resolved / (resist[rows, lanes] + jnp.abs(resolved))
                amounts[rows, lanes] = jnp.abs(slip)
                sums = [sums[c] + parts[c] * slip for c in range(6)]
            return tuple(trial[c] - 2.0 * sums[c] for c in range(6))

        now = lax.fori_loop(0, ITERS, sweep, tuple(trial))
        for c in range(6):
            stress_out[points * c : points * (c + 1), lanes] = now[c]
        return carry

    lax.fori_loop(0, items // LANES, tile_step, 0)
    amount = amounts[...]
    high, low = two_terms(amount)
    harden = product(harden_map[...], jnp.concatenate([high, low, high], axis=0))
    grown = resist[...] + HARDENING * harden
    resist_out[...] = grown
    work = grown * amount
    stored = work[:points]
    for a in range(1, systems):
        stored = stored + work[points * a : points * (a + 1)]
    prolonged(stored, repeat[...], spread[...], energy)


def phase_kernel(
    grains,
    x_before,
    x_after,
    z_before,
    z_after,
    energy,
    mobility,
    grain_state,
    out,
    x_first,
    x_last,
    z_first,
    z_last,
):
    orders, size_x, size_z, size_y = grains.shape
    row = lax.broadcasted_iota(jnp.int32, (size_z, size_y), 0)
    for x in range(size_x):
        center = [grains[order, x] for order in range(orders)]
        squares = [value * value for value in center]
        total = squares[0]
        for order in range(1, orders):
            total = total + squares[order]
        shared = 2.0 * CROSS_TERM * total + 5.0
        cell = energy[x // 2]
        for order in range(orders):
            value = center[order]
            lower = grains[order, x - 1] if x > 0 else x_before[order]
            upper = grains[order, x + 1] if x < size_x - 1 else x_after[order]
            below = jnp.where(
                row == 0, z_before[order, x : x + 1], pltpu.roll(value, 1, 0)
            )
            above = jnp.where(
                row == size_z - 1,
                z_after[order, x : x + 1],
                pltpu.roll(value, size_z - 1, 0),
            )
            around = (
                (lower + upper)
                + (below + above)
                + (pltpu.roll(value, 1, 1) + pltpu.roll(value, size_y - 1, 1))
            )
            share = 2.0 * DRIVE_SCALE * (1.0 - grain_state[order])
            factor = shared + share * cell - 2.0 * squares[order]
            new = value + (TIME_STEP * mobility[order]) * (around - value * factor)
            out[order, x] = new
            if x == 0:
                x_first[order] = new
            if x == size_x - 1:
                x_last[order] = new
            z_first[order, x : x + 1] = new[:1]
            z_last[order, x : x + 1] = new[size_z - 1 :]


def neighbours(first, last, axis):
    size = lax.axis_size(axis)
    up = [(i, (i + 1) % size) for i in range(size)]
    down = [(j, i) for i, j in up]
    return lax.ppermute(last, axis, up), lax.ppermute(first, axis, down)


def pair_rank(owners, count_all):
    onehot = (owners[:, None] == jnp.arange(count_all, dtype=jnp.int32)[None, :]).astype(jnp.int32)
    before = jnp.cumsum(onehot, axis=0) - onehot
    return jnp.sum(before * onehot, axis=1)


def over_points(matrix, points):
    rows, columns = matrix.shape
    same = jnp.eye(points, dtype=F32)
    spread = matrix[:, None, :, None] * same[None, :, None, :]
    return spread.reshape(rows * points, columns * points)


def shards(
    grains,
    block_owner,
    element_anchor,
    strain_step,
    stress,
    resistance,
    slip_active,
    orientation_schmid,
    latent_hardening,
    mobility,
    grain_state,
):
    count_all = lax.axis_size(("gx", "gz"))
    owners = block_owner.reshape(-1)
    per_dev = owners.shape[0]
    capacity = 2 * per_dev // count_all
    slots_all = count_all * capacity
    orders, size_x, size_z, size_y = grains.shape
    points = stress.shape[1]
    systems = resistance.shape[0]
    tensors, forces = 6 * points, systems * points
    wide = -(-(2 * tensors + forces + systems) // LANES) * LANES
    narrow = -(-(tensors + forces) // LANES) * LANES

    outbox = call(pack_state_kernel, shape(slots_all, wide))(
        element_anchor.reshape(1, per_dev),
        strain_step.reshape(tensors, per_dev),
        stress.reshape(tensors, per_dev),
        resistance.reshape(forces, per_dev),
        slip_active,
    )
    inbox = routed(outbox)

    mailbox = owners * capacity + pair_rank(owners, count_all)
    mailbox_col = jnp.broadcast_to(mailbox[:, None], (per_dev, LANES))
    anchor_col = jnp.broadcast_to(element_anchor[:, None], (per_dev, LANES))
    schmid = orientation_schmid.reshape(orders, systems * 6).T
    schmid_high, schmid_low = two_terms_outside(schmid)
    tensor_map = jnp.concatenate(
        [over_points(part, points).astype(BF16) for part in (schmid_high, schmid_high, schmid_low)],
        axis=1,
    )
    harden_high, harden_low = two_terms_outside(latent_hardening)
    harden_map = jnp.concatenate(
        [over_points(part, points).astype(BF16) for part in (harden_high, harden_high, harden_low)],
        axis=1,
    )
    active_map = jnp.repeat(jnp.eye(systems, dtype=F32), points, axis=0).astype(BF16)
    rows, lanes = row_map(), lane_map(size_y)
    repeat, spread = repeat_map(), spread_map(size_y)

    edges = (grains[:, 0], grains[:, size_x - 1], grains[:, :, 0], grains[:, :, size_z - 1])
    strain_h = stress_h = resist_h = active_h = None
    scalars = pl.BlockSpec(memory_space=pltpu.SMEM)
    whole = pl.BlockSpec(memory_space=pltpu.VMEM)
    for cycle in range(STEPS):
        x_before, x_after = neighbours(edges[0], edges[1], "gx")
        z_before, z_after = neighbours(edges[2], edges[3], "gz")
        weights = call(restrict_kernel, shape(orders * points, per_dev))(grains, rows, lanes)
        if cycle == 0:
            strain_h, stress_h, resist_h, active_h = call(
                unpack_state_kernel,
                (
                    shape(tensors, per_dev),
                    shape(tensors, per_dev),
                    shape(forces, per_dev),
                    shape(systems, per_dev),
                ),
            )(mailbox_col, inbox)
        stress_h, resist_h, energy = call(
            mechanics_kernel,
            (
                shape(tensors, per_dev),
                shape(forces, per_dev),
                shape(size_x // 2, size_z, size_y),
            ),
            scratch=(
                pltpu.VMEM((6 * forces, per_dev), F32),
                pltpu.VMEM((forces, per_dev), F32),
                pltpu.VMEM((forces, per_dev), F32),
            ),
        )(
            weights,
            strain_h,
            stress_h,
            resist_h,
            active_h,
            tensor_map,
            harden_map,
            active_map,
            repeat,
            spread,
        )
        for inner in range(SUB):
            if inner > 0:
                x_before, x_after = neighbours(edges[0], edges[1], "gx")
                z_before, z_after = neighbours(edges[2], edges[3], "gz")
            grains, *edges = call(
                phase_kernel,
                (
                    shape(orders, size_x, size_z, size_y),
                    shape(orders, size_z, size_y),
                    shape(orders, size_z, size_y),
                    shape(orders, size_x, size_y),
                    shape(orders, size_x, size_y),
                ),
                in_specs=[whole] * 6 + [scalars] * 2,
            )(grains, x_before, x_after, z_before, z_after, energy, mobility, grain_state)
    outbox = call(pack_result_kernel, shape(slots_all, narrow))(
        mailbox.reshape(1, per_dev), stress_h, resist_h
    )
    inbox = routed(outbox)
    stress, resistance = call(
        unpack_result_kernel, (shape(tensors, per_dev), shape(forces, per_dev))
    )(anchor_col, inbox)
    return (
        grains,
        stress.reshape(6, points, per_dev),
        resistance.reshape(systems, points, per_dev),
    )


def solution(mesh):
    return jax.shard_map(
        shards,
        mesh=mesh,
        in_specs=(
            P(None, "gx", "gz", None),
            P("gx", "gz", None),
            P(("gx", "gz")),
            P(None, None, ("gx", "gz")),
            P(None, None, ("gx", "gz")),
            P(None, None, ("gx", "gz")),
            P(None, ("gx", "gz")),
            P(),
            P(),
            P(),
            P(),
        ),
        out_specs=(
            P(None, "gx", "gz", None),
            P(None, None, ("gx", "gz")),
            P(None, None, ("gx", "gz")),
        ),
        check_vma=False,
    )
```

```python
import functools

import jax
import jax.numpy as jnp
from jax import lax
from jax.experimental import pallas as pl
from jax.experimental.pallas import tpu as pltpu
from jax.sharding import PartitionSpec as P

ITERS = 4
STEPS = 3
SUB = 2

CROSS_TERM = 1.5
DRIVE_SCALE = 6.0
TIME_STEP = 0.02
SLIP_RATE = 0.1
HARDENING = 0.5
LANES = 128
BF16 = jnp.bfloat16
F32 = jnp.float32


def two_terms(value):
    high = value.astype(BF16)
    low = (value - high.astype(F32)).astype(BF16)
    return high, low


def product(left, right):
    return lax.dot_general(
        left, right, (((1,), (0,)), ((), ())), preferred_element_type=F32
    )


def product_rows(left, right):
    return lax.dot_general(
        left, right, (((1,), (1,)), ((), ())), preferred_element_type=F32
    )


def call(kernel, shapes, limit, scratch=(), **options):
    return pl.pallas_call(
        kernel,
        out_shape=shapes,
        scratch_shapes=list(scratch),
        compiler_params=pltpu.CompilerParams(vmem_limit_bytes=limit and limit << 20),
        **options,
    )


def shape(*dims):
    return jax.ShapeDtypeStruct(dims, F32)


def hit_rows(slots_row, slot):
    return (slot == slots_row).astype(F32).astype(BF16)


def into_slots(hit, values):
    high, low = two_terms(values)
    return product_rows(hit, high) + product_rows(hit, low)


def hit_columns(slots_col, count):
    lane = lax.broadcasted_iota(jnp.int32, (slots_col.shape[0], LANES), 1)
    return jnp.concatenate(
        [
            (lane + start == slots_col).astype(F32).astype(BF16)
            for start in range(0, count, LANES)
        ],
        axis=1,
    )


def out_of_slots(hit, mail):
    high, low = two_terms(mail)
    return product(hit, high) + product(hit, low)


def pack_state_kernel(
    anchor, strain, stress, resist, active, out, values, flags, wide_mail, rest_mail, sems
):
    tensors, forces = strain.shape[0], resist.shape[0]
    copies = [
        pltpu.make_async_copy(resist, values.at[2 * tensors : 2 * tensors + forces], sems.at[0]),
        pltpu.make_async_copy(strain, values.at[:tensors], sems.at[1]),
        pltpu.make_async_copy(stress, values.at[tensors : 2 * tensors], sems.at[2]),
        pltpu.make_async_copy(active, flags, sems.at[3]),
    ]
    for copy in copies:
        copy.start()
    items = values.shape[1]
    slots_all = wide_mail.shape[0]
    slots_row = anchor[...]
    slot = lax.broadcasted_iota(jnp.int32, (slots_all, items), 0)
    hit = hit_rows(slots_row, slot)
    row = lax.broadcasted_iota(jnp.int32, (slots_all // 2, items), 0)
    lower = (row >> 2) * 8 + (row & 3)
    sides = jnp.concatenate([hit_rows(slots_row, lower), hit_rows(slots_row, lower + 4)], axis=1)
    for copy in copies:
        copy.wait()
    wide_mail[...] = into_slots(hit, values[: 2 * LANES])
    total = 2 * tensors + forces
    rest = jnp.concatenate(
        [values[2 * LANES : total], flags[...].astype(F32), jnp.zeros((8, items), F32)], axis=0
    )
    empty = jnp.zeros_like(rest)
    both = jnp.concatenate(
        [jnp.concatenate([rest, empty], axis=1), jnp.concatenate([empty, rest], axis=1)], axis=0
    )
    rest_mail[...] = into_slots(sides, both)
    upper = lax.broadcasted_iota(jnp.int32, (8, LANES), 0) < 4
    for pair in range(slots_all // 16):
        start = 16 * pair
        left = pltpu.roll(wide_mail[start + 8 : start + 16, :LANES], 4, 0)
        right = pltpu.roll(wide_mail[start + 8 : start + 16, LANES:], 4, 0)
        side = rest_mail[8 * pair : 8 * pair + 8]
        out[40 * pair : 40 * pair + 8] = wide_mail[start : start + 8, :LANES]
        out[40 * pair + 8 : 40 * pair + 16] = wide_mail[start : start + 8, LANES:]
        out[40 * pair + 16 : 40 * pair + 24] = jnp.where(upper, side, left)
        out[40 * pair + 24 : 40 * pair + 32] = jnp.where(upper, left, right)
        out[40 * pair + 32 : 40 * pair + 40] = jnp.where(upper, right, side)


def unpack_state_kernel(
    mailbox, mail, strain, stress, resist, active, wide_mail, rest_mail
):
    slots_all = wide_mail.shape[0]
    upper = lax.broadcasted_iota(jnp.int32, (8, LANES), 0) < 4
    for pair in range(slots_all // 16):
        start = 16 * pair
        third, fourth, fifth = (
            mail[40 * pair + 8 * k : 40 * pair + 8 * k + 8] for k in (2, 3, 4)
        )
        wide_mail[start : start + 8, :LANES] = mail[40 * pair : 40 * pair + 8]
        wide_mail[start : start + 8, LANES:] = mail[40 * pair + 8 : 40 * pair + 16]
        wide_mail[start + 8 : start + 16, :LANES] = pltpu.roll(
            jnp.where(upper, fourth, third), 4, 0
        )
        wide_mail[start + 8 : start + 16, LANES:] = pltpu.roll(
            jnp.where(upper, fifth, fourth), 4, 0
        )
        rest_mail[8 * pair : 8 * pair + 8] = jnp.where(upper, third, fifth)
    slots = mailbox[...]
    wide = out_of_slots(hit_columns(slots, slots_all), wide_mail[...])
    row = (slots >> 3) * 4 + (slots & 3)
    rest = out_of_slots(hit_columns(row, slots_all // 2), rest_mail[...])
    rest = jnp.where((slots & 4) > 0, pltpu.roll(rest, LANES // 2, 1), rest)
    values = jnp.transpose(jnp.concatenate([wide, rest], axis=1))
    start = 0
    for part in (strain, stress, resist, active):
        part[...] = values[start : start + part.shape[0]]
        start += part.shape[0]


def pack_result_kernel(mailbox, stress, resist, out):
    rows = stress.shape[0] + resist.shape[0]
    values = jnp.concatenate(
        [
            stress[...],
            resist[...],
            jnp.zeros((out.shape[1] - rows, stress.shape[1]), F32),
        ],
        axis=0,
    )
    slot = lax.broadcasted_iota(jnp.int32, (out.shape[0], values.shape[1]), 0)
    out[...] = into_slots(hit_rows(mailbox[...], slot), values)


def unpack_result_kernel(anchor, mail, stress, resist):
    values = jnp.transpose(out_of_slots(hit_columns(anchor[...], mail.shape[0]), mail[...]))
    stress[...] = values[: stress.shape[0]]
    resist[...] = values[stress.shape[0] : stress.shape[0] + resist.shape[0]]


def exchanged(sent):
    return lax.all_to_all(sent, ("gx", "gz"), split_axis=0, concat_axis=0, tiled=True)


def grid_of(rows, columns):
    dims = (rows, columns)
    return lax.broadcasted_iota(jnp.int32, dims, 0), lax.broadcasted_iota(jnp.int32, dims, 1)


def marked(condition, value=1.0):
    return jnp.where(condition, value, 0.0).astype(BF16)


def field(index, low, width):
    return (index >> low) & ((1 << width) - 1)


def row_map():
    to, index = grid_of(128, 256)
    same = (
        (field(to, 6, 1) == field(index, 2, 1))
        & (field(to, 5, 1) == field(index, 6, 1))
        & (field(to, 4, 1) == field(index, 5, 1))
        & (field(to, 3, 1) == field(index, 3, 1))
        & (field(to, 2, 1) == field(index, 4, 1))
        & (field(to, 1, 1) == field(index, 1, 1))
    )
    return marked(same, 0.125)


def lane_map():
    index, to = grid_of(1024, 256)
    y = field(index, 0, 8)
    return marked(
        ((y >> 2) == field(to, 0, 6))
        & (field(y, 1, 1) == field(to, 7, 1))
        & (field(index, 8, 1) == field(to, 6, 1))
    )


def spread_map():
    index, y = grid_of(512, 256)
    return marked(((y >> 2) == field(index, 0, 6)) & (field(y, 1, 1) == field(index, 7, 1)))


def repeat_map():
    to, index = grid_of(32, 16)
    return marked(
        (field(to, 4, 1) == field(index, 0, 1))
        & (field(to, 3, 1) == field(index, 2, 1))
        & (field(to, 1, 1) == field(index, 1, 1))
    )


def over_points(matrix):
    rows, columns = matrix.shape
    wide = columns * 8
    high, low = two_terms(matrix)
    index, to = grid_of(columns, 3 * wide)
    source = (to >> 3) - jnp.where(to >= wide, columns, 0) - jnp.where(to >= 2 * wide, columns, 0)
    same = index == source
    spread = product(high, marked(same & (to < 2 * wide))) + product(
        low, marked(same & (to >= 2 * wide))
    )
    to, index = grid_of(rows * 8, rows)
    tall = product(marked((to >> 3) == index), spread.astype(BF16))
    row, column = grid_of(rows * 8, 3 * wide)
    return jnp.where((row & 7) == (column & 7), tall, 0.0).astype(BF16)


def column_of(row):
    tall = jnp.broadcast_to(row.astype(F32), (LANES, row.shape[1]))
    return jnp.transpose(tall).astype(jnp.int32)


def prepare_kernel(
    owner,
    anchor,
    schmid,
    latent,
    mailbox_row,
    mailbox_col,
    anchor_col,
    tensor_map,
    harden_map,
    active_map,
    rows,
    lanes,
    repeat,
    spread,
):
    owners = jnp.concatenate(
        [owner[i, j : j + 1] for i in range(owner.shape[0]) for j in range(owner.shape[1])],
        axis=1,
    )
    items = owners.shape[1]
    device = lax.broadcasted_iota(jnp.int32, (128, items), 0)
    onehot = (device == owners).astype(F32)
    index, to = grid_of(items, items)
    before = product(onehot.astype(BF16), marked(index < to))
    rank = jnp.sum(before * onehot, axis=0, keepdims=True).astype(jnp.int32)
    mailbox = owners * 8 + rank
    mailbox_row[...] = mailbox
    mailbox_col[...] = column_of(mailbox)
    anchor_col[...] = column_of(anchor[...])
    tensor_map[...] = over_points(schmid[...])
    harden_map[...] = over_points(latent[...])
    to, index = grid_of(active_map.shape[0], active_map.shape[1])
    active_map[...] = marked((to >> 3) == index)
    rows[...] = row_map()
    lanes[...] = lane_map()
    repeat[...] = repeat_map()
    spread[...] = spread_map()


def restrict_kernel(grains, rows, lanes, weights):
    orders, size_x, size_z, size_y = grains.shape
    lefts = []
    for pair in range(orders // 2):
        parts = []
        for order in (2 * pair, 2 * pair + 1):
            for coarse in range(size_x // 2):
                low = grains[order, 2 * coarse]
                high = grains[order, 2 * coarse + 1]
                parts.append(low * low + high * high)
        summed = jnp.concatenate(parts, axis=0)
        moved = product(rows[...], jnp.concatenate(two_terms(summed), axis=0))
        high, low = two_terms(moved)
        lefts.append(
            jnp.concatenate([high[:64], high[64:], low[:64], low[64:]], axis=1)
        )
    found = product(jnp.concatenate(lefts, axis=0), lanes[...])
    row = lax.broadcasted_iota(jnp.int32, (found.shape[0], LANES), 0)
    picked = jnp.where(row % 2 == 0, found[:, :LANES], found[:, LANES:])
    for order in range(orders):
        for tile in range(4):
            start = (order * 4 + tile) * 8
            weights[order * 8 : order * 8 + 8, tile * LANES : (tile + 1) * LANES] = picked[
                start : start + 8
            ]


def prolonged(stored, repeat, spread, energy):
    high, low = two_terms(stored)
    rows = product(repeat, jnp.concatenate([high, low], axis=0))
    row = lax.broadcasted_iota(jnp.int32, rows.shape, 0)
    lane = lax.broadcasted_iota(jnp.int32, rows.shape, 1)
    rows = jnp.where((row // 4) % 2 == (lane // 64) % 2, rows, 0.0)
    tiles = [
        jnp.concatenate(
            [rows[:16, t * LANES : (t + 1) * LANES], rows[16:, t * LANES : (t + 1) * LANES]],
            axis=1,
        )
        for t in range(4)
    ]
    left = jnp.concatenate(two_terms(jnp.concatenate(tiles, axis=0)), axis=1)
    cells = product(left, spread)
    for bx in range(2):
        for pair in range(2):
            for qx in range(2):
                start = ((bx * 2 + pair) * 2 + qx) * 8
                energy[bx * 2 + qx, pair * 8 : pair * 8 + 8] = cells[start : start + 8]


def mechanics_kernel(
    weights,
    strain,
    stress,
    resist,
    active,
    tensor_map,
    harden_map,
    active_map,
    repeat,
    spread,
    stress_out,
    resist_out,
    energy,
    tensor,
    rates,
    amounts,
):
    systems = active.shape[0]
    points = resist.shape[0] // systems
    items = weights.shape[1]
    high, low = two_terms(weights[...])
    tensor[...] = product(tensor_map[...], jnp.concatenate([high, low, high], axis=0))
    rates[...] = product(active_map[...], active[...].astype(BF16)) * SLIP_RATE

    def tile_step(tile, carry):
        lanes = pl.ds(pl.multiple_of(tile * LANES, LANES), LANES)
        trial = [
            stress[points * c : points * (c + 1), lanes]
            + 2.0 * strain[points * c : points * (c + 1), lanes]
            for c in range(6)
        ]

        def sweep(_, now):
            sums = [jnp.zeros((points, LANES), F32) for _ in range(6)]
            for a in range(systems):
                rows = pl.ds(a * points, points)
                parts = [tensor[pl.ds((a * 6 + c) * points, points), lanes] for c in range(6)]
                resolved = (
                    (parts[0] * now[0] + parts[1] * now[1])
                    + (parts[2] * now[2] + parts[3] * now[3])
                    + (parts[4] * now[4] + parts[5] * now[5])
                )
                slip = rates[rows, lanes] * resolved / (resist[rows, lanes] + jnp.abs(resolved))
                amounts[rows, lanes] = jnp.abs(slip)
                sums = [sums[c] + parts[c] * slip for c in range(6)]
            return tuple(trial[c] - 2.0 * sums[c] for c in range(6))

        now = lax.fori_loop(0, ITERS, sweep, tuple(trial))
        for c in range(6):
            stress_out[points * c : points * (c + 1), lanes] = now[c]
        return carry

    lax.fori_loop(0, items // LANES, tile_step, 0)
    amount = amounts[...]
    high, low = two_terms(amount)
    harden = product(harden_map[...], jnp.concatenate([high, low, high], axis=0))
    grown = resist[...] + HARDENING * harden
    resist_out[...] = grown
    work = grown * amount
    stored = work[:points]
    for a in range(1, systems):
        stored = stored + work[points * a : points * (a + 1)]
    prolonged(stored, repeat[...], spread[...], energy)


def own_and_other(odd, even_value, odd_value):
    return jnp.where(odd > 0, odd_value, even_value)


def new_layer(grains, x, lower, upper, z_pair, z_other, energy, odd_z, mobility, grain_state):
    orders, _, size_z, size_y = grains.shape
    row = lax.broadcasted_iota(jnp.int32, (size_z, size_y), 0)
    center = [grains[order, x] for order in range(orders)]
    squares = [value * value for value in center]
    total = squares[0]
    for order in range(1, orders):
        total = total + squares[order]
    shared = 2.0 * CROSS_TERM * total + 5.0
    cell = energy[x // 2]
    found = []
    for order in range(orders):
        value = center[order]
        z_mate, z_next = z_pair[order, x : x + 1], z_other[order, x : x + 1]
        below = jnp.where(row == 0, own_and_other(odd_z, z_next, z_mate), pltpu.roll(value, 1, 0))
        above = jnp.where(
            row == size_z - 1,
            own_and_other(odd_z, z_mate, z_next),
            pltpu.roll(value, size_z - 1, 0),
        )
        around = (
            (lower(order) + upper(order))
            + (below + above)
            + (pltpu.roll(value, 1, 1) + pltpu.roll(value, size_y - 1, 1))
        )
        share = 2.0 * DRIVE_SCALE * (1.0 - grain_state[order])
        factor = shared + share * cell - 2.0 * squares[order]
        found.append(value + (TIME_STEP * mobility[order]) * (around - value * factor))
    return found


def new_ends(grains, x_pair, x_other, odd_x, *others):
    last = grains.shape[1] - 1
    low = new_layer(
        grains,
        0,
        lambda order: own_and_other(odd_x, x_other[order], x_pair[order]),
        lambda order: grains[order, 1],
        *others,
    )
    high = new_layer(
        grains,
        last,
        lambda order: grains[order, last - 1],
        lambda order: own_and_other(odd_x, x_pair[order], x_other[order]),
        *others,
    )
    return low, high


def new_inner(grains, x, *others):
    return new_layer(
        grains,
        x,
        lambda order: grains[order, x - 1],
        lambda order: grains[order, x + 1],
        *others,
    )


def send_layers(odd_x, order, low, high, x_pair, x_other):
    x_pair[order] = own_and_other(odd_x, high, low)
    x_other[order] = own_and_other(odd_x, low, high)


def send_rows(odd_z, order, x, new, z_pair, z_other):
    size_z = new.shape[0]
    first, last = new[:1], new[size_z - 1 :]
    z_pair[order, x : x + 1] = own_and_other(odd_z, last, first)
    z_other[order, x : x + 1] = own_and_other(odd_z, first, last)


def edges_kernel(grains, odd, x_pair, x_other, z_pair, z_other):
    orders, size_x, _, _ = grains.shape
    for order in range(orders):
        send_layers(
            odd[0], order, grains[order, 0], grains[order, size_x - 1], x_pair, x_other
        )
        for x in range(size_x):
            send_rows(odd[1], order, x, grains[order, x], z_pair, z_other)


def first_ends_kernel(
    grains,
    x_pair,
    x_other,
    z_pair,
    z_other,
    energy,
    odd,
    mobility,
    grain_state,
    x_pair_out,
    x_other_out,
):
    low, high = new_ends(
        grains, x_pair, x_other, odd[0], z_pair, z_other, energy, odd[1], mobility, grain_state
    )
    for order in range(grains.shape[0]):
        send_layers(odd[0], order, low[order], high[order], x_pair_out, x_other_out)


def first_inner_kernel(
    grains,
    z_pair,
    z_other,
    energy,
    x_pair_new,
    x_other_new,
    odd,
    mobility,
    grain_state,
    out,
    z_pair_out,
    z_other_out,
):
    orders, size_x, _, _ = grains.shape
    for order in range(orders):
        low = own_and_other(odd[0], x_other_new[order], x_pair_new[order])
        high = own_and_other(odd[0], x_pair_new[order], x_other_new[order])
        for x, new in ((0, low), (size_x - 1, high)):
            out[order, x] = new
            send_rows(odd[1], order, x, new, z_pair_out, z_other_out)
    for x in range(1, size_x - 1):
        found = new_inner(grains, x, z_pair, z_other, energy, odd[1], mobility, grain_state)
        for order in range(orders):
            out[order, x] = found[order]
            send_rows(odd[1], order, x, found[order], z_pair_out, z_other_out)


def second_inner_kernel(grains, z_pair, z_other, energy, odd, mobility, grain_state, out):
    orders, size_x, _, _ = grains.shape
    for x in range(1, size_x - 1):
        found = new_inner(grains, x, z_pair, z_other, energy, odd[1], mobility, grain_state)
        for order in range(orders):
            out[order, x] = found[order]


def second_ends_kernel(
    grains,
    x_pair,
    x_other,
    z_pair,
    z_other,
    energy,
    inner,
    odd,
    mobility,
    grain_state,
    out,
    x_pair_out,
    x_other_out,
    z_pair_out,
    z_other_out,
):
    orders, size_x, _, _ = grains.shape
    low, high = new_ends(
        grains, x_pair, x_other, odd[0], z_pair, z_other, energy, odd[1], mobility, grain_state
    )
    for order in range(orders):
        send_layers(odd[0], order, low[order], high[order], x_pair_out, x_other_out)
        for x, new in ((0, low[order]), (size_x - 1, high[order])):
            out[order, x] = new
            send_rows(odd[1], order, x, new, z_pair_out, z_other_out)
        for x in range(1, size_x - 1):
            send_rows(odd[1], order, x, inner[order, x], z_pair_out, z_other_out)


def last_inner_kernel(
    grains, z_pair, z_other, energy, odd, mobility, grain_state, out, held, sems
):
    orders, size_x, _, _ = grains.shape
    copies = []
    for x in range(1, size_x - 1):
        found = new_inner(grains, x, z_pair, z_other, energy, odd[1], mobility, grain_state)
        for order in range(orders):
            held[x - 1, order] = found[order]
        copies.append(pltpu.make_async_copy(held.at[x - 1], out.at[:, x], sems.at[x - 1]))
        copies[-1].start()
    for copy in copies:
        copy.wait()


def last_ends_kernel(
    grains,
    x_pair,
    x_other,
    z_pair,
    z_other,
    energy,
    inner,
    odd,
    mobility,
    grain_state,
    out,
    held,
    sems,
):
    orders, size_x, _, _ = grains.shape
    ends = new_ends(
        grains, x_pair, x_other, odd[0], z_pair, z_other, energy, odd[1], mobility, grain_state
    )
    copies = []
    for side, x in ((0, 0), (1, size_x - 1)):
        for order in range(orders):
            held[side, order] = ends[side][order]
        copies.append(pltpu.make_async_copy(held.at[side], out.at[:, x], sems.at[side]))
        copies[-1].start()
    for copy in copies:
        copy.wait()


def swapped(value, axis, first):
    size = lax.axis_size(axis)
    pairs = [(i % size, (i + 1) % size) for i in range(first, size + first, 2)]
    return lax.ppermute(value, axis, pairs + [(j, i) for i, j in pairs])


def halos(edges):
    return (
        swapped(edges[0], "gx", 0),
        swapped(edges[1], "gx", 1),
        swapped(edges[2], "gz", 0),
        swapped(edges[3], "gz", 1),
    )


def shards(
    grains,
    block_owner,
    element_anchor,
    strain_step,
    stress,
    resistance,
    slip_active,
    orientation_schmid,
    latent_hardening,
    mobility,
    grain_state,
):
    count_all = lax.axis_size(("gx", "gz"))
    per_dev = element_anchor.shape[0]
    slots_all = 2 * per_dev
    orders, size_x, size_z, size_y = grains.shape
    points = stress.shape[1]
    systems = resistance.shape[0]
    tensors, forces = 6 * points, systems * points
    narrow = -(-(tensors + forces) // LANES) * LANES
    scalars = pl.BlockSpec(memory_space=pltpu.SMEM)
    whole = pl.BlockSpec(memory_space=pltpu.VMEM)
    far = pl.BlockSpec(memory_space=pltpu.HBM)
    anchor = element_anchor.reshape(1, per_dev)
    message = 5 * slots_all // 2

    outbox = call(
        pack_state_kernel,
        shape(message, LANES),
        limit=None,
        scratch=(
            pltpu.VMEM((2 * tensors + forces, per_dev), F32),
            pltpu.VMEM((systems, per_dev), jnp.int32),
            pltpu.VMEM((slots_all, 2 * LANES), F32),
            pltpu.VMEM((slots_all // 2, LANES), F32),
            pltpu.SemaphoreType.DMA((4,)),
        ),
        in_specs=[whole, far, far, far, far],
    )(
        anchor,
        strain_step.reshape(tensors, per_dev),
        stress.reshape(tensors, per_dev),
        resistance.reshape(forces, per_dev),
        slip_active,
    )
    inbox = exchanged(outbox.reshape(count_all, 5, 4, LANES)).reshape(message, LANES)

    whole_number = functools.partial(jax.ShapeDtypeStruct, dtype=jnp.int32)
    half_wide = functools.partial(jax.ShapeDtypeStruct, dtype=BF16)
    (
        mailbox_row,
        mailbox_col,
        anchor_col,
        tensor_map,
        harden_map,
        active_map,
        rows,
        lanes,
        repeat,
        spread,
    ) = call(
        prepare_kernel,
        (
            whole_number((1, per_dev)),
            whole_number((per_dev, LANES)),
            whole_number((per_dev, LANES)),
            half_wide((6 * forces, 3 * orders * points)),
            half_wide((forces, 3 * forces)),
            half_wide((forces, systems)),
            half_wide((128, 256)),
            half_wide((1024, 256)),
            half_wide((32, 16)),
            half_wide((512, 256)),
        ),
        limit=12,
    )(
        block_owner,
        anchor,
        orientation_schmid.reshape(orders, systems * 6).T,
        latent_hardening,
    )
    odd = jnp.stack([lax.axis_index("gx") % 2, lax.axis_index("gz") % 2]).astype(jnp.int32)
    edge_shapes = (
        shape(orders, size_z, size_y),
        shape(orders, size_z, size_y),
        shape(orders, size_x, size_y),
        shape(orders, size_x, size_y),
    )
    edges = call(edges_kernel, edge_shapes, limit=4, in_specs=[whole, scalars])(grains, odd)
    strain_h = stress_h = resist_h = active_h = None
    for cycle in range(STEPS):
        around = halos(edges)
        weights = call(restrict_kernel, shape(orders * points, per_dev), limit=8)(
            grains, rows, lanes
        )
        if cycle == 0:
            strain_h, stress_h, resist_h, active_h = call(
                unpack_state_kernel,
                (
                    shape(tensors, per_dev),
                    shape(tensors, per_dev),
                    shape(forces, per_dev),
                    shape(systems, per_dev),
                ),
                limit=16,
                scratch=(
                    pltpu.VMEM((slots_all, 2 * LANES), F32),
                    pltpu.VMEM((slots_all // 2, LANES), F32),
                ),
            )(mailbox_col, inbox)
        stress_h, resist_h, energy = call(
            mechanics_kernel,
            (
                shape(tensors, per_dev),
                shape(forces, per_dev),
                shape(size_x // 2, size_z, size_y),
            ),
            limit=12,
            scratch=(
                pltpu.VMEM((6 * forces, per_dev), F32),
                pltpu.VMEM((forces, per_dev), F32),
                pltpu.VMEM((forces, per_dev), F32),
            ),
        )(
            weights,
            strain_h,
            stress_h,
            resist_h,
            active_h,
            tensor_map,
            harden_map,
            active_map,
            repeat,
            spread,
        )
        if cycle == STEPS - 1:
            around, stress_h = lax.optimization_barrier((around, stress_h))
        brick = shape(orders, size_x, size_z, size_y)
        tables = (odd, mobility, grain_state)
        x_pair, x_other = call(
            first_ends_kernel, edge_shapes[:2], limit=4, in_specs=[whole] * 6 + [scalars] * 3
        )(grains, *around, energy, *tables)
        grains, z_pair, z_other = call(
            first_inner_kernel,
            (brick,) + edge_shapes[2:],
            limit=4,
            in_specs=[whole] * 6 + [scalars] * 3,
        )(grains, *around[2:], energy, x_pair, x_other, *tables)
        around = halos((x_pair, x_other, z_pair, z_other))
        if cycle < STEPS - 1:
            inner = call(
                second_inner_kernel, brick, limit=4, in_specs=[whole] * 4 + [scalars] * 3
            )(grains, *around[2:], energy, *tables)
            grains, *edges = call(
                second_ends_kernel,
                (brick,) + edge_shapes,
                limit=4,
                in_specs=[whole] * 7 + [scalars] * 3,
                input_output_aliases={6: 0},
            )(grains, *around, energy, inner, *tables)
        else:
            inner = call(
                last_inner_kernel,
                brick,
                limit=6,
                in_specs=[whole] * 4 + [scalars] * 3,
                out_specs=far,
                scratch=(
                    pltpu.VMEM((size_x - 2, orders, size_z, size_y), F32),
                    pltpu.SemaphoreType.DMA((size_x - 2,)),
                ),
            )(grains, *around[2:], energy, *tables)
            last = (grains, *around, energy, inner, *tables)
    outbox = call(pack_result_kernel, shape(slots_all, narrow), limit=12)(
        mailbox_row, stress_h, resist_h
    )
    inbox = exchanged(outbox.reshape(count_all, slots_all // count_all, narrow))
    stress, resistance = call(
        unpack_result_kernel, (shape(tensors, per_dev), shape(forces, per_dev)), limit=12
    )(anchor_col, inbox.reshape(slots_all, narrow))
    last, stress, resistance = lax.optimization_barrier((last, stress, resistance))
    grains = call(
        last_ends_kernel,
        brick,
        limit=4,
        in_specs=[whole] * 6 + [far] + [scalars] * 3,
        out_specs=far,
        scratch=(
            pltpu.VMEM((2, orders, size_z, size_y), F32),
            pltpu.SemaphoreType.DMA((2,)),
        ),
        input_output_aliases={6: 0},
    )(*last)
    return (
        grains,
        stress.reshape(6, points, per_dev),
        resistance.reshape(systems, points, per_dev),
    )


def solution(mesh):
    return jax.shard_map(
        shards,
        mesh=mesh,
        in_specs=(
            P(None, "gx", "gz", None),
            P("gx", "gz", None),
            P(("gx", "gz")),
            P(None, None, ("gx", "gz")),
            P(None, None, ("gx", "gz")),
            P(None, None, ("gx", "gz")),
            P(None, ("gx", "gz")),
            P(),
            P(),
            P(),
            P(),
        ),
        out_specs=(
            P(None, "gx", "gz", None),
            P(None, None, ("gx", "gz")),
            P(None, None, ("gx", "gz")),
        ),
        check_vma=False,
    )
```

```python
import functools

import jax
import jax.numpy as jnp
from jax import lax
from jax.experimental import pallas as pl
from jax.experimental.pallas import tpu as pltpu
from jax.sharding import PartitionSpec as P

ITERS = 4
STEPS = 3
SUB = 2

CROSS_TERM = 1.5
DRIVE_SCALE = 6.0
TIME_STEP = 0.02
SLIP_RATE = 0.1
HARDENING = 0.5
LANES = 128
WIDE = 256
CHUNKS = 4
BF16 = jnp.bfloat16
F32 = jnp.float32


def two_terms(value):
    high = value.astype(BF16)
    low = (value - high.astype(F32)).astype(BF16)
    return high, low


def product(left, right):
    return lax.dot_general(
        left, right, (((1,), (0,)), ((), ())), preferred_element_type=F32
    )


def product_rows(left, right):
    return lax.dot_general(
        left, right, (((1,), (1,)), ((), ())), preferred_element_type=F32
    )


def call(kernel, shapes, limit, scratch=(), **options):
    return pl.pallas_call(
        kernel,
        out_shape=shapes,
        scratch_shapes=list(scratch),
        compiler_params=pltpu.CompilerParams(vmem_limit_bytes=limit and limit << 20),
        **options,
    )


def shape(*dims):
    return jax.ShapeDtypeStruct(dims, F32)


def hit_rows(slots_row, slot):
    return (slot == slots_row).astype(F32).astype(BF16)


def into_slots(hit, values):
    high, low = two_terms(values)
    return product_rows(hit, high) + product_rows(hit, low)


def hit_columns(slots_col, count):
    lane = lax.broadcasted_iota(jnp.int32, (slots_col.shape[0], LANES), 1)
    return jnp.concatenate(
        [
            (lane + start == slots_col).astype(F32).astype(BF16)
            for start in range(0, count, LANES)
        ],
        axis=1,
    )


def out_of_slots(hit, mail):
    high, low = two_terms(mail)
    return product(hit, high) + product(hit, low)


def pack_state_kernel(
    anchor, strain, stress, resist, active, out, values, flags, wide_mail, rest_mail, mail, sems
):
    tensors, forces = strain.shape[0], resist.shape[0]
    copies = [
        pltpu.make_async_copy(resist, values.at[2 * tensors : 2 * tensors + forces], sems.at[0]),
        pltpu.make_async_copy(strain, values.at[:tensors], sems.at[1]),
        pltpu.make_async_copy(stress, values.at[tensors : 2 * tensors], sems.at[2]),
        pltpu.make_async_copy(active, flags, sems.at[3]),
    ]
    for copy in copies:
        copy.start()
    items = values.shape[1]
    slots_all = wide_mail.shape[0]
    slots_row = anchor[...]
    slot = lax.broadcasted_iota(jnp.int32, (slots_all, items), 0)
    hit = hit_rows(slots_row, slot)
    for copy in copies:
        copy.wait()
    total = 2 * tensors + forces
    rest = jnp.concatenate(
        [values[2 * LANES : total], flags[...].astype(F32), jnp.zeros((8, items), F32)], axis=0
    )
    rest = jnp.concatenate(two_terms(rest), axis=0)
    wide = two_terms(values[: 2 * LANES])
    upper = lax.broadcasted_iota(jnp.int32, (8, LANES), 0) < 4
    near = lax.broadcasted_iota(jnp.int32, (8, LANES), 1) < LANES // 2
    part = slots_all // CHUNKS
    sent = []
    for chunk in range(CHUNKS):
        rows = slice(chunk * part, (chunk + 1) * part)
        wide_mail[rows] = product_rows(hit[rows], wide[0]) + product_rows(hit[rows], wide[1])
        terms = product_rows(hit[rows], rest)
        rest_mail[rows] = terms + pltpu.roll(terms, LANES // 2, 1)
        for pair in range(chunk * part // 16, (chunk + 1) * part // 16):
            start = 16 * pair
            left = pltpu.roll(wide_mail[start + 8 : start + 16, :LANES], 4, 0)
            right = pltpu.roll(wide_mail[start + 8 : start + 16, LANES:], 4, 0)
            one, two = rest_mail[start : start + 8], rest_mail[start + 8 : start + 16]
            side = jnp.where(
                upper,
                jnp.where(near, one, pltpu.roll(one, 4, 0)),
                jnp.where(near, pltpu.roll(two, 4, 0), two),
            )
            mail[40 * pair : 40 * pair + 8] = wide_mail[start : start + 8, :LANES]
            mail[40 * pair + 8 : 40 * pair + 16] = wide_mail[start : start + 8, LANES:]
            mail[40 * pair + 16 : 40 * pair + 24] = jnp.where(upper, side, left)
            mail[40 * pair + 24 : 40 * pair + 32] = jnp.where(upper, left, right)
            mail[40 * pair + 32 : 40 * pair + 40] = jnp.where(upper, right, side)
        rows = slice(chunk * part * 5 // 2, (chunk + 1) * part * 5 // 2)
        sent.append(pltpu.make_async_copy(mail.at[rows], out.at[rows], sems.at[4 + chunk]))
        sent[-1].start()
    for copy in sent:
        copy.wait()


def unpack_state_kernel(
    mailbox, mail, strain, stress, resist, active, wide_mail, rest_mail, slots_row, sem
):
    fetch = pltpu.make_async_copy(mailbox, slots_row, sem)
    fetch.start()
    slots_all = wide_mail.shape[0]
    upper = lax.broadcasted_iota(jnp.int32, (8, LANES), 0) < 4
    for pair in range(slots_all // 16):
        start = 16 * pair
        third, fourth, fifth = (
            mail[40 * pair + 8 * k : 40 * pair + 8 * k + 8] for k in (2, 3, 4)
        )
        wide_mail[start : start + 8, :LANES] = mail[40 * pair : 40 * pair + 8]
        wide_mail[start : start + 8, LANES:] = mail[40 * pair + 8 : 40 * pair + 16]
        wide_mail[start + 8 : start + 16, :LANES] = pltpu.roll(
            jnp.where(upper, fourth, third), 4, 0
        )
        wide_mail[start + 8 : start + 16, LANES:] = pltpu.roll(
            jnp.where(upper, fifth, fourth), 4, 0
        )
        rest_mail[8 * pair : 8 * pair + 8] = jnp.where(upper, third, fifth)
    wide_terms, rest_terms = two_terms(wide_mail[...]), two_terms(rest_mail[...])
    fetch.wait()
    slots = column_of(slots_row[...])
    hit = hit_columns(slots, slots_all)
    wide = product(hit, wide_terms[0]) + product(hit, wide_terms[1])
    row = (slots >> 3) * 4 + (slots & 3)
    hit = hit_columns(row, slots_all // 2)
    rest = product(hit, jnp.concatenate(rest_terms, axis=1))
    rest = rest[:, :LANES] + rest[:, LANES:]
    rest = jnp.where((slots & 4) > 0, pltpu.roll(rest, LANES // 2, 1), rest)
    values = jnp.transpose(jnp.concatenate([wide, rest], axis=1))
    start = 0
    for part in (strain, stress, resist, active):
        part[...] = values[start : start + part.shape[0]]
        start += part.shape[0]


def pack_result_kernel(mailbox, stress, resist, out, mail, sems):
    rows = stress.shape[0] + resist.shape[0]
    values = jnp.concatenate(
        [
            stress[...],
            resist[...],
            jnp.zeros((out.shape[1] - rows, stress.shape[1]), F32),
        ],
        axis=0,
    )
    high, low = two_terms(values)
    part = out.shape[0] // CHUNKS
    slot = lax.broadcasted_iota(jnp.int32, (part, values.shape[1]), 0)
    sent = []
    for chunk in range(CHUNKS):
        rows = slice(chunk * part, (chunk + 1) * part)
        hit = hit_rows(mailbox[...] - chunk * part, slot)
        mail[rows] = product_rows(hit, high) + product_rows(hit, low)
        sent.append(pltpu.make_async_copy(mail.at[rows], out.at[rows], sems.at[chunk]))
        sent[-1].start()
    for copy in sent:
        copy.wait()


def unpack_result_kernel(anchor, mail, stress, resist):
    hit = hit_columns(column_of(anchor[...]), mail.shape[0])
    values = jnp.transpose(out_of_slots(hit, mail[...]))
    stress[...] = values[: stress.shape[0]]
    resist[...] = values[stress.shape[0] : stress.shape[0] + resist.shape[0]]


def exchanged(sent):
    return lax.all_to_all(sent, ("gx", "gz"), split_axis=0, concat_axis=0, tiled=True)


def grid_of(rows, columns):
    dims = (rows, columns)
    return lax.broadcasted_iota(jnp.int32, dims, 0), lax.broadcasted_iota(jnp.int32, dims, 1)


def marked(condition, value=1.0):
    return jnp.where(condition, value, 0.0).astype(BF16)


def field(index, low, width):
    return (index >> low) & ((1 << width) - 1)


def row_map():
    to, index = grid_of(128, 256)
    same = (
        (field(to, 6, 1) == field(index, 2, 1))
        & (field(to, 5, 1) == field(index, 6, 1))
        & (field(to, 4, 1) == field(index, 5, 1))
        & (field(to, 3, 1) == field(index, 3, 1))
        & (field(to, 2, 1) == field(index, 4, 1))
        & (field(to, 1, 1) == field(index, 1, 1))
    )
    return marked(same, 0.125)


def lane_map():
    index, to = grid_of(512, 256)
    y = field(index, 0, 8)
    return marked(
        ((y >> 2) == field(to, 0, 6))
        & (field(y, 1, 1) == field(to, 7, 1))
        & (field(index, 8, 1) == field(to, 6, 1))
    )


def spread_map():
    index, y = grid_of(256, 256)
    return marked(((y >> 2) == field(index, 0, 6)) & (field(y, 1, 1) == field(index, 7, 1)))


def repeat_map():
    to, index = grid_of(32, 16)
    return marked(
        (field(to, 4, 1) == field(index, 0, 1))
        & (field(to, 3, 1) == field(index, 2, 1))
        & (field(to, 1, 1) == field(index, 1, 1))
    )


def over_points(matrix):
    rows, columns = matrix.shape
    wide = columns * 8
    high, low = two_terms(matrix)
    index, to = grid_of(columns, 3 * wide)
    source = (to >> 3) - jnp.where(to >= wide, columns, 0) - jnp.where(to >= 2 * wide, columns, 0)
    same = index == source
    spread = product(high, marked(same & (to < 2 * wide))) + product(
        low, marked(same & (to >= 2 * wide))
    )
    to, index = grid_of(rows * 8, rows)
    tall = product(marked((to >> 3) == index), spread.astype(BF16))
    row, column = grid_of(rows * 8, 3 * wide)
    return jnp.where((row & 7) == (column & 7), tall, 0.0).astype(BF16)


def column_of(row):
    tall = jnp.broadcast_to(row.astype(F32), (LANES, row.shape[1]))
    return jnp.transpose(tall).astype(jnp.int32)


def prepare_kernel(
    owner,
    schmid,
    latent,
    places,
    mailbox_row,
    tensor_map,
    harden_map,
    active_map,
    rows,
    lanes,
    repeat,
    spread,
    table,
):
    table[...] = jnp.broadcast_to(places[...], table.shape)
    owners = jnp.concatenate(
        [owner[i, j : j + 1] for i in range(owner.shape[0]) for j in range(owner.shape[1])],
        axis=1,
    )
    items = owners.shape[1]
    device = lax.broadcasted_iota(jnp.int32, (128, items), 0)
    onehot = (device == owners).astype(F32)
    index, to = grid_of(items, items)
    before = product(onehot.astype(BF16), marked(index < to))
    rank = jnp.sum(before * onehot, axis=0, keepdims=True).astype(jnp.int32)
    mailbox = owners * 8 + rank
    mailbox_row[...] = mailbox
    tensor_map[...] = over_points(schmid[...])
    harden_map[...] = over_points(latent[...])
    to, index = grid_of(active_map.shape[0], active_map.shape[1])
    active_map[...] = marked((to >> 3) == index)
    rows[...] = row_map()
    lanes[...] = lane_map()
    repeat[...] = repeat_map()
    spread[...] = spread_map()


def restrict_kernel(grains, rows, lanes, weights):
    orders, size_x, size_z, size_y = grains.shape
    lefts = ([], [])
    for pair in range(orders // 2):
        parts = []
        for order in (2 * pair, 2 * pair + 1):
            for coarse in range(size_x // 2):
                low = grains[order, 2 * coarse]
                high = grains[order, 2 * coarse + 1]
                parts.append(low * low + high * high)
        summed = jnp.concatenate(parts, axis=0)
        moved = product(rows[...], jnp.concatenate(two_terms(summed), axis=0))
        for left, part in zip(lefts, two_terms(moved)):
            left.append(jnp.concatenate([part[:64], part[64:]], axis=1))
    found = product(jnp.concatenate(lefts[0], axis=0), lanes[...])
    found = found + product(jnp.concatenate(lefts[1], axis=0), lanes[...])
    row = lax.broadcasted_iota(jnp.int32, (found.shape[0], LANES), 0)
    picked = jnp.where(row % 2 == 0, found[:, :LANES], found[:, LANES:])
    for order in range(orders):
        for tile in range(4):
            start = (order * 4 + tile) * 8
            weights[order * 8 : order * 8 + 8, tile * LANES : (tile + 1) * LANES] = picked[
                start : start + 8
            ]


def prolonged(stored, repeat, spread, energy):
    high, low = two_terms(stored)
    rows = product(repeat, jnp.concatenate([high, low], axis=0))
    row = lax.broadcasted_iota(jnp.int32, rows.shape, 0)
    lane = lax.broadcasted_iota(jnp.int32, rows.shape, 1)
    rows = jnp.where((row // 4) % 2 == (lane // 64) % 2, rows, 0.0)
    tiles = [
        jnp.concatenate(
            [rows[:16, t * LANES : (t + 1) * LANES], rows[16:, t * LANES : (t + 1) * LANES]],
            axis=1,
        )
        for t in range(4)
    ]
    high, low = two_terms(jnp.concatenate(tiles, axis=0))
    cells = product(high, spread) + product(low, spread)
    for bx in range(2):
        for pair in range(2):
            for qx in range(2):
                start = ((bx * 2 + pair) * 2 + qx) * 8
                energy[bx * 2 + qx, pair * 8 : pair * 8 + 8] = cells[start : start + 8]


def mechanics_kernel(
    weights,
    strain,
    stress,
    resist,
    active,
    tensor_map,
    harden_map,
    active_map,
    repeat,
    spread,
    stress_out,
    resist_out,
    energy,
    tensor,
    rates,
    amounts,
):
    systems = active.shape[0]
    points = resist.shape[0] // systems
    items = weights.shape[1]
    high, low = two_terms(weights[...])
    tensor[...] = product(tensor_map[...], jnp.concatenate([high, low, high], axis=0))
    rates[...] = product(active_map[...], active[...].astype(BF16)) * SLIP_RATE

    def tile_step(tile, carry):
        lanes = pl.ds(pl.multiple_of(tile * WIDE, WIDE), WIDE)
        trial = [
            stress[points * c : points * (c + 1), lanes]
            + 2.0 * strain[points * c : points * (c + 1), lanes]
            for c in range(6)
        ]

        def sweep(_, now):
            sums = [jnp.zeros((points, WIDE), F32) for _ in range(6)]
            for a in range(systems):
                rows = pl.ds(a * points, points)
                parts = [tensor[pl.ds((a * 6 + c) * points, points), lanes] for c in range(6)]
                resolved = (
                    (parts[0] * now[0] + parts[1] * now[1])
                    + (parts[2] * now[2] + parts[3] * now[3])
                    + (parts[4] * now[4] + parts[5] * now[5])
                )
                slip = rates[rows, lanes] * resolved / (resist[rows, lanes] + jnp.abs(resolved))
                amounts[rows, lanes] = jnp.abs(slip)
                sums = [sums[c] + parts[c] * slip for c in range(6)]
            return tuple(trial[c] - 2.0 * sums[c] for c in range(6))

        now = lax.fori_loop(0, ITERS, sweep, tuple(trial))
        for c in range(6):
            stress_out[points * c : points * (c + 1), lanes] = now[c]
        return carry

    lax.fori_loop(0, items // WIDE, tile_step, 0)
    amount = amounts[...]
    high, low = two_terms(amount)
    harden = product(harden_map[...], jnp.concatenate([high, low, high], axis=0))
    grown = resist[...] + HARDENING * harden
    resist_out[...] = grown
    work = grown * amount
    stored = work[:points]
    for a in range(1, systems):
        stored = stored + work[points * a : points * (a + 1)]
    prolonged(stored, repeat[...], spread[...], energy)


def own_and_other(odd, even_value, odd_value):
    return jnp.where(odd > 0.0, odd_value, even_value)


def odd_x_of(table):
    return table[16:17]


def odd_z_of(table):
    return table[17:18]


def z_rows(table, order, x, z_pair, z_other):
    odd_z = odd_z_of(table)
    mate, other = z_pair[order, x : x + 1], z_other[order, x : x + 1]
    return own_and_other(odd_z, other, mate), own_and_other(odd_z, mate, other)


def new_layer(grains, x, lower, upper, z_pair, z_other, energy, table):
    orders, _, size_z, size_y = grains.shape
    row = lax.broadcasted_iota(jnp.int32, (size_z, size_y), 0)
    center = [grains[order, x] for order in range(orders)]
    squares = [value * value for value in center]
    total = squares[0]
    for order in range(1, orders):
        total = total + squares[order]
    shared = 2.0 * CROSS_TERM * total + 5.0
    cell = energy[x // 2]
    found = []
    for order in range(orders):
        value = center[order]
        first, last = 0.0, 0.0
        if z_pair is not None:
            first, last = z_rows(table, order, x, z_pair, z_other)
        below = jnp.where(row == 0, first, pltpu.roll(value, 1, 0))
        above = jnp.where(row == size_z - 1, last, pltpu.roll(value, size_z - 1, 0))
        around = (
            (lower(order) + upper(order))
            + (below + above)
            + (pltpu.roll(value, 1, 1) + pltpu.roll(value, size_y - 1, 1))
        )
        factor = shared + table[8 + order : 9 + order] * cell - 2.0 * squares[order]
        found.append(value + table[order : order + 1] * (around - value * factor))
    return found


def new_ends(grains, x_pair, x_other, odd_x, *others):
    last = grains.shape[1] - 1
    low = new_layer(
        grains,
        0,
        lambda order: own_and_other(odd_x, x_other[order], x_pair[order]),
        lambda order: grains[order, 1],
        *others,
    )
    high = new_layer(
        grains,
        last,
        lambda order: grains[order, last - 1],
        lambda order: own_and_other(odd_x, x_pair[order], x_other[order]),
        *others,
    )
    return low, high


def new_inner(grains, x, *others):
    return new_layer(
        grains,
        x,
        lambda order: grains[order, x - 1],
        lambda order: grains[order, x + 1],
        *others,
    )


def send_layers(odd_x, order, low, high, x_pair, x_other):
    x_pair[order] = own_and_other(odd_x, high, low)
    x_other[order] = own_and_other(odd_x, low, high)


def send_rows(odd_z, order, x, new, z_pair, z_other):
    size_z = new.shape[0]
    first, last = new[:1], new[size_z - 1 :]
    z_pair[order, x : x + 1] = own_and_other(odd_z, last, first)
    z_other[order, x : x + 1] = own_and_other(odd_z, first, last)


def edges_kernel(grains, table, x_pair, x_other, z_pair, z_other):
    orders, size_x, _, _ = grains.shape
    for order in range(orders):
        send_layers(
            odd_x_of(table), order, grains[order, 0], grains[order, size_x - 1], x_pair, x_other
        )
        for x in range(size_x):
            send_rows(odd_z_of(table), order, x, grains[order, x], z_pair, z_other)


def ends_kernel(
    grains,
    x_pair,
    x_other,
    z_pair,
    z_other,
    energy,
    table,
    x_pair_out,
    x_other_out,
):
    low, high = new_ends(
        grains, x_pair, x_other, odd_x_of(table), z_pair, z_other, energy, table
    )
    for order in range(grains.shape[0]):
        send_layers(odd_x_of(table), order, low[order], high[order], x_pair_out, x_other_out)


def first_inner_kernel(
    grains,
    z_pair,
    z_other,
    energy,
    x_pair_new,
    x_other_new,
    table,
    out,
    z_pair_out,
    z_other_out,
):
    orders, size_x, _, _ = grains.shape
    for order in range(orders):
        low = own_and_other(odd_x_of(table), x_other_new[order], x_pair_new[order])
        high = own_and_other(odd_x_of(table), x_pair_new[order], x_other_new[order])
        for x, new in ((0, low), (size_x - 1, high)):
            out[order, x] = new
            send_rows(odd_z_of(table), order, x, new, z_pair_out, z_other_out)
    for x in range(1, size_x - 1):
        found = new_inner(grains, x, z_pair, z_other, energy, table)
        for order in range(orders):
            out[order, x] = found[order]
            send_rows(odd_z_of(table), order, x, found[order], z_pair_out, z_other_out)


def second_inner_kernel(grains, energy, table, out):
    orders, size_x, _, _ = grains.shape
    for x in range(1, size_x - 1):
        found = new_inner(grains, x, None, None, energy, table)
        for order in range(orders):
            out[order, x] = found[order]


def end_rows(inner, order, x, z_pair, z_other, table):
    size_z = inner.shape[2]
    first, last = z_rows(table, order, x, z_pair, z_other)
    step = table[order : order + 1]
    return (
        inner[order, x, :1] + step * first,
        inner[order, x, size_z - 1 :] + step * last,
    )


def second_rows_kernel(
    inner, x_pair_new, x_other_new, z_pair, z_other, table, out, z_pair_out, z_other_out
):
    orders, size_x, size_z, _ = inner.shape
    odd_x, odd_z = odd_x_of(table), odd_z_of(table)
    for order in range(orders):
        low = own_and_other(odd_x, x_other_new[order], x_pair_new[order])
        high = own_and_other(odd_x, x_pair_new[order], x_other_new[order])
        for x, new in ((0, low), (size_x - 1, high)):
            out[order, x] = new
            send_rows(odd_z, order, x, new, z_pair_out, z_other_out)
        for x in range(1, size_x - 1):
            first, last = end_rows(inner, order, x, z_pair, z_other, table)
            out[order, x, :1] = first
            out[order, x, size_z - 1 :] = last
            z_pair_out[order, x : x + 1] = own_and_other(odd_z, last, first)
            z_other_out[order, x : x + 1] = own_and_other(odd_z, first, last)


def last_rows_kernel(inner, z_pair, z_other, table, out, held, sem):
    orders, size_x, size_z, _ = inner.shape
    for order in range(orders):
        for x in range(1, size_x - 1):
            first, last = end_rows(inner, order, x, z_pair, z_other, table)
            held[order, x] = inner[order, x]
            held[order, x, :1] = first
            held[order, x, size_z - 1 :] = last
    inside = (slice(None), slice(1, size_x - 1))
    copy = pltpu.make_async_copy(held.at[inside], out.at[inside], sem)
    copy.start()
    copy.wait()


def last_ends_kernel(
    grains, x_pair, x_other, z_pair, z_other, energy, table, inner, out, held, sems
):
    size_x = grains.shape[1]
    ends = new_ends(grains, x_pair, x_other, odd_x_of(table), z_pair, z_other, energy, table)
    copies = []
    for side, x in ((0, 0), (1, size_x - 1)):
        for order in range(grains.shape[0]):
            held[side, order] = ends[side][order]
        copies.append(pltpu.make_async_copy(held.at[side], out.at[:, x], sems.at[side]))
        copies[-1].start()
    for copy in copies:
        copy.wait()


def swapped(value, axis, first):
    size = lax.axis_size(axis)
    pairs = [(i % size, (i + 1) % size) for i in range(first, size + first, 2)]
    return lax.ppermute(value, axis, pairs + [(j, i) for i, j in pairs])


def halos(edges):
    x_other = swapped(edges[1], "gx", 1)
    z_other = swapped(edges[3], "gz", 1)
    x_pair = swapped(edges[0], "gx", 0)
    z_pair = swapped(edges[2], "gz", 0)
    return x_pair, x_other, z_pair, z_other


def shards(
    grains,
    block_owner,
    element_anchor,
    strain_step,
    stress,
    resistance,
    slip_active,
    orientation_schmid,
    latent_hardening,
    mobility,
    grain_state,
):
    count_all = lax.axis_size(("gx", "gz"))
    per_dev = element_anchor.shape[0]
    slots_all = 2 * per_dev
    orders, size_x, size_z, size_y = grains.shape
    points = stress.shape[1]
    systems = resistance.shape[0]
    tensors, forces = 6 * points, systems * points
    narrow = -(-(tensors + forces) // LANES) * LANES
    whole = pl.BlockSpec(memory_space=pltpu.VMEM)
    far = pl.BlockSpec(memory_space=pltpu.HBM)
    anchor = element_anchor.reshape(1, per_dev)
    message = 5 * slots_all // 2

    outbox = call(
        pack_state_kernel,
        shape(message, LANES),
        limit=None,
        scratch=(
            pltpu.VMEM((2 * tensors + forces, per_dev), F32),
            pltpu.VMEM((systems, per_dev), jnp.int32),
            pltpu.VMEM((slots_all, 2 * LANES), F32),
            pltpu.VMEM((slots_all, LANES), F32),
            pltpu.VMEM((message, LANES), F32),
            pltpu.SemaphoreType.DMA((4 + CHUNKS,)),
        ),
        in_specs=[whole, far, far, far, far],
        out_specs=far,
    )(
        anchor,
        strain_step.reshape(tensors, per_dev),
        stress.reshape(tensors, per_dev),
        resistance.reshape(forces, per_dev),
        slip_active,
    )
    inbox = exchanged(outbox.reshape(count_all, 5, 4, LANES)).reshape(message, LANES)

    places = jnp.concatenate(
        [
            TIME_STEP * mobility,
            2.0 * DRIVE_SCALE * (1.0 - grain_state),
            jnp.stack([lax.axis_index(name) % 2 for name in ("gx", "gz")]).astype(F32),
            jnp.zeros((6,), F32),
        ]
    ).reshape(24, 1)
    whole_number = functools.partial(jax.ShapeDtypeStruct, dtype=jnp.int32)
    half_wide = functools.partial(jax.ShapeDtypeStruct, dtype=BF16)
    (
        mailbox_row,
        tensor_map,
        harden_map,
        active_map,
        rows,
        lanes,
        repeat,
        spread,
        table,
    ) = call(
        prepare_kernel,
        (
            whole_number((1, per_dev)),
            half_wide((6 * forces, 3 * orders * points)),
            half_wide((forces, 3 * forces)),
            half_wide((forces, systems)),
            half_wide((128, 256)),
            half_wide((512, 256)),
            half_wide((32, 16)),
            half_wide((256, 256)),
            shape(24, size_y),
        ),
        limit=12,
    )(
        block_owner,
        orientation_schmid.reshape(orders, systems * 6).T,
        latent_hardening,
        places,
    )
    edge_shapes = (
        shape(orders, size_z, size_y),
        shape(orders, size_z, size_y),
        shape(orders, size_x, size_y),
        shape(orders, size_x, size_y),
    )
    edges = call(edges_kernel, edge_shapes, limit=4, in_specs=[whole] * 2)(grains, table)
    strain_h = stress_h = resist_h = active_h = None
    for cycle in range(STEPS):
        around = halos(edges)
        weights = call(restrict_kernel, shape(orders * points, per_dev), limit=8)(
            grains, rows, lanes
        )
        if cycle == 0:
            strain_h, stress_h, resist_h, active_h = call(
                unpack_state_kernel,
                (
                    shape(tensors, per_dev),
                    shape(tensors, per_dev),
                    shape(forces, per_dev),
                    shape(systems, per_dev),
                ),
                limit=16,
                in_specs=[far, whole],
                scratch=(
                    pltpu.VMEM((slots_all, 2 * LANES), F32),
                    pltpu.VMEM((slots_all // 2, LANES), F32),
                    pltpu.VMEM((1, per_dev), jnp.int32),
                    pltpu.SemaphoreType.DMA,
                ),
            )(mailbox_row, inbox)
        stress_h, resist_h, energy = call(
            mechanics_kernel,
            (
                shape(tensors, per_dev),
                shape(forces, per_dev),
                shape(size_x // 2, size_z, size_y),
            ),
            limit=12,
            scratch=(
                pltpu.VMEM((6 * forces, per_dev), F32),
                pltpu.VMEM((forces, per_dev), F32),
                pltpu.VMEM((forces, per_dev), F32),
            ),
        )(
            weights,
            strain_h,
            stress_h,
            resist_h,
            active_h,
            tensor_map,
            harden_map,
            active_map,
            repeat,
            spread,
        )
        if cycle == STEPS - 1:
            around, stress_h = lax.optimization_barrier((around, stress_h))
        brick = shape(orders, size_x, size_z, size_y)
        x_pair, x_other = call(
            ends_kernel, edge_shapes[:2], limit=4, in_specs=[whole] * 7
        )(grains, *around, energy, table)
        grains, z_pair, z_other = call(
            first_inner_kernel,
            (brick,) + edge_shapes[2:],
            limit=4,
            in_specs=[whole] * 7,
        )(grains, *around[2:], energy, x_pair, x_other, table)
        around = halos((x_pair, x_other, z_pair, z_other))
        inner = call(
            second_inner_kernel,
            brick,
            limit=4,
            in_specs=[whole] * 3,
            out_specs=whole,
        )(grains, energy, table)
        if cycle < STEPS - 1:
            x_pair, x_other = call(
                ends_kernel, edge_shapes[:2], limit=4, in_specs=[whole] * 7
            )(grains, *around, energy, table)
            grains, z_pair, z_other = call(
                second_rows_kernel,
                (brick,) + edge_shapes[2:],
                limit=4,
                in_specs=[whole] * 6,
                out_specs=[whole] * 3,
                input_output_aliases={0: 0},
            )(inner, x_pair, x_other, *around[2:], table)
            edges = (x_pair, x_other, z_pair, z_other)
    outbox = call(
        pack_result_kernel,
        shape(slots_all, narrow),
        limit=12,
        out_specs=far,
        scratch=(pltpu.VMEM((slots_all, narrow), F32), pltpu.SemaphoreType.DMA((CHUNKS,))),
    )(
        mailbox_row, stress_h, resist_h
    )
    inbox = exchanged(outbox.reshape(count_all, slots_all // count_all, narrow))
    inside = call(
        last_rows_kernel,
        brick,
        limit=4,
        in_specs=[whole] * 4,
        out_specs=far,
        scratch=(
            pltpu.VMEM((orders, size_x, size_z, size_y), F32),
            pltpu.SemaphoreType.DMA,
        ),
    )(inner, *around[2:], table)
    grains = call(
        last_ends_kernel,
        brick,
        limit=4,
        in_specs=[whole] * 7 + [far],
        out_specs=far,
        scratch=(
            pltpu.VMEM((2, orders, size_z, size_y), F32),
            pltpu.SemaphoreType.DMA((2,)),
        ),
        input_output_aliases={7: 0},
    )(grains, *around, energy, table, inside)
    grains, inbox = lax.optimization_barrier((grains, inbox))
    stress, resistance = call(
        unpack_result_kernel, (shape(tensors, per_dev), shape(forces, per_dev)), limit=12
    )(anchor, inbox.reshape(slots_all, narrow))
    return (
        grains,
        stress.reshape(6, points, per_dev),
        resistance.reshape(systems, points, per_dev),
    )


def solution(mesh):
    return jax.shard_map(
        shards,
        mesh=mesh,
        in_specs=(
            P(None, "gx", "gz", None),
            P("gx", "gz", None),
            P(("gx", "gz")),
            P(None, None, ("gx", "gz")),
            P(None, None, ("gx", "gz")),
            P(None, None, ("gx", "gz")),
            P(None, ("gx", "gz")),
            P(),
            P(),
            P(),
            P(),
        ),
        out_specs=(
            P(None, "gx", "gz", None),
            P(None, None, ("gx", "gz")),
            P(None, None, ("gx", "gz")),
        ),
        check_vma=False,
    )
```

```python
import functools

import jax
import jax.numpy as jnp
from jax import lax
from jax.experimental import pallas as pl
from jax.experimental.pallas import tpu as pltpu
from jax.sharding import PartitionSpec as P


ITERS = 4
STEPS = 3

CROSS_TERM = 1.5
DRIVE_SCALE = 6.0
TIME_STEP = 0.02
SLIP_RATE = 0.1
HARDENING = 0.5
LANES = 128
WIDE = 256
CHUNKS = 4
BF16 = jnp.bfloat16
F32 = jnp.float32


def two_terms(value):
    high = value.astype(BF16)
    low = (value - high.astype(F32)).astype(BF16)
    return high, low


def product(left, right):
    return lax.dot_general(
        left, right, (((1,), (0,)), ((), ())), preferred_element_type=F32
    )


def product_rows(left, right):
    return lax.dot_general(
        left, right, (((1,), (1,)), ((), ())), preferred_element_type=F32
    )


def call(kernel, shapes, limit, scratch=(), **options):
    return pl.pallas_call(
        kernel,
        out_shape=shapes,
        scratch_shapes=list(scratch),
        compiler_params=pltpu.CompilerParams(vmem_limit_bytes=limit and limit << 20),
        **options,
    )


def shape(*dims):
    return jax.ShapeDtypeStruct(dims, F32)


def hit_rows(slots_row, slot):
    return (slot == slots_row).astype(F32).astype(BF16)


def hit_columns(slots_col, count):
    lane = lax.broadcasted_iota(jnp.int32, (slots_col.shape[0], LANES), 1)
    return jnp.concatenate(
        [
            (lane + start == slots_col).astype(F32).astype(BF16)
            for start in range(0, count, LANES)
        ],
        axis=1,
    )


def out_of_slots(hit, mail):
    high, low = two_terms(mail)
    return product(hit, high) + product(hit, low)


def pack_state_kernel(
    anchor, strain, stress, resist, active, out, values, flags, wide_mail, rest_mail, mail, sems
):
    tensors, forces = strain.shape[0], resist.shape[0]
    copies = [
        pltpu.make_async_copy(resist, values.at[2 * tensors : 2 * tensors + forces], sems.at[0]),
        pltpu.make_async_copy(strain, values.at[:tensors], sems.at[1]),
        pltpu.make_async_copy(stress, values.at[tensors : 2 * tensors], sems.at[2]),
        pltpu.make_async_copy(active, flags, sems.at[3]),
    ]
    for copy in copies:
        copy.start()
    items = values.shape[1]
    slots_all = wide_mail.shape[0]
    slots_row = anchor[...]
    slot = lax.broadcasted_iota(jnp.int32, (slots_all, items), 0)
    hit = hit_rows(slots_row, slot)
    for copy in copies:
        copy.wait()
    total = 2 * tensors + forces
    rest = jnp.concatenate(
        [values[2 * LANES : total], flags[...].astype(F32), jnp.zeros((8, items), F32)], axis=0
    )
    rest = jnp.concatenate(two_terms(rest), axis=0)
    wide = two_terms(values[: 2 * LANES])
    upper = lax.broadcasted_iota(jnp.int32, (8, LANES), 0) < 4
    near = lax.broadcasted_iota(jnp.int32, (8, LANES), 1) < LANES // 2
    part = slots_all // CHUNKS
    sent = []
    for chunk in range(CHUNKS):
        rows = slice(chunk * part, (chunk + 1) * part)
        wide_mail[rows] = product_rows(hit[rows], wide[0]) + product_rows(hit[rows], wide[1])
        terms = product_rows(hit[rows], rest)
        rest_mail[rows] = terms + pltpu.roll(terms, LANES // 2, 1)
        for pair in range(chunk * part // 16, (chunk + 1) * part // 16):
            start = 16 * pair
            left = pltpu.roll(wide_mail[start + 8 : start + 16, :LANES], 4, 0)
            right = pltpu.roll(wide_mail[start + 8 : start + 16, LANES:], 4, 0)
            one, two = rest_mail[start : start + 8], rest_mail[start + 8 : start + 16]
            side = jnp.where(
                upper,
                jnp.where(near, one, pltpu.roll(one, 4, 0)),
                jnp.where(near, pltpu.roll(two, 4, 0), two),
            )
            mail[40 * pair : 40 * pair + 8] = wide_mail[start : start + 8, :LANES]
            mail[40 * pair + 8 : 40 * pair + 16] = wide_mail[start : start + 8, LANES:]
            mail[40 * pair + 16 : 40 * pair + 24] = jnp.where(upper, side, left)
            mail[40 * pair + 24 : 40 * pair + 32] = jnp.where(upper, left, right)
            mail[40 * pair + 32 : 40 * pair + 40] = jnp.where(upper, right, side)
        rows = slice(chunk * part * 5 // 2, (chunk + 1) * part * 5 // 2)
        sent.append(pltpu.make_async_copy(mail.at[rows], out.at[rows], sems.at[4 + chunk]))
        sent[-1].start()
    for copy in sent:
        copy.wait()


def unpack_state_kernel(
    mailbox, mail, strain, stress, resist, active, wide_mail, rest_mail, slots_row, sem
):
    fetch = pltpu.make_async_copy(mailbox, slots_row, sem)
    fetch.start()
    slots_all = wide_mail.shape[0]
    upper = lax.broadcasted_iota(jnp.int32, (8, LANES), 0) < 4
    for pair in range(slots_all // 16):
        start = 16 * pair
        third, fourth, fifth = (
            mail[40 * pair + 8 * k : 40 * pair + 8 * k + 8] for k in (2, 3, 4)
        )
        wide_mail[start : start + 8, :LANES] = mail[40 * pair : 40 * pair + 8]
        wide_mail[start : start + 8, LANES:] = mail[40 * pair + 8 : 40 * pair + 16]
        wide_mail[start + 8 : start + 16, :LANES] = pltpu.roll(
            jnp.where(upper, fourth, third), 4, 0
        )
        wide_mail[start + 8 : start + 16, LANES:] = pltpu.roll(
            jnp.where(upper, fifth, fourth), 4, 0
        )
        rest_mail[8 * pair : 8 * pair + 8] = jnp.where(upper, third, fifth)
    wide_terms, rest_terms = two_terms(wide_mail[...]), two_terms(rest_mail[...])
    fetch.wait()
    slots = column_of(slots_row[...])
    hit = hit_columns(slots, slots_all)
    wide = product(hit, wide_terms[0]) + product(hit, wide_terms[1])
    row = (slots >> 3) * 4 + (slots & 3)
    hit = hit_columns(row, slots_all // 2)
    rest = product(hit, jnp.concatenate(rest_terms, axis=1))
    rest = rest[:, :LANES] + rest[:, LANES:]
    rest = jnp.where((slots & 4) > 0, pltpu.roll(rest, LANES // 2, 1), rest)
    values = jnp.transpose(jnp.concatenate([wide, rest], axis=1))
    start = 0
    for part in (strain, stress, resist, active):
        part[...] = values[start : start + part.shape[0]]
        start += part.shape[0]


def pack_result_kernel(mailbox, stress, resist, out, mail, sems):
    rows = stress.shape[0] + resist.shape[0]
    values = jnp.concatenate(
        [
            stress[...],
            resist[...],
            jnp.zeros((out.shape[1] - rows, stress.shape[1]), F32),
        ],
        axis=0,
    )
    high, low = two_terms(values)
    part = out.shape[0] // CHUNKS
    slot = lax.broadcasted_iota(jnp.int32, (part, values.shape[1]), 0)
    sent = []
    for chunk in range(CHUNKS):
        rows = slice(chunk * part, (chunk + 1) * part)
        hit = hit_rows(mailbox[...] - chunk * part, slot)
        mail[rows] = product_rows(hit, high) + product_rows(hit, low)
        sent.append(pltpu.make_async_copy(mail.at[rows], out.at[rows], sems.at[chunk]))
        sent[-1].start()
    for copy in sent:
        copy.wait()


def unpack_result_kernel(anchor, mail, stress, resist):
    hit = hit_columns(column_of(anchor[...]), mail.shape[0])
    values = jnp.transpose(out_of_slots(hit, mail[...]))
    stress[...] = values[: stress.shape[0]]
    resist[...] = values[stress.shape[0] : stress.shape[0] + resist.shape[0]]


def exchanged(sent):
    return lax.all_to_all(sent, ("gx", "gz"), split_axis=0, concat_axis=0, tiled=True)


def grid_of(rows, columns):
    dims = (rows, columns)
    return lax.broadcasted_iota(jnp.int32, dims, 0), lax.broadcasted_iota(jnp.int32, dims, 1)


def marked(condition, value=1.0):
    return jnp.where(condition, value, 0.0).astype(BF16)


def field(index, low, width):
    return (index >> low) & ((1 << width) - 1)


def row_map():
    to, index = grid_of(128, 256)
    same = (
        (field(to, 6, 1) == field(index, 2, 1))
        & (field(to, 5, 1) == field(index, 6, 1))
        & (field(to, 4, 1) == field(index, 5, 1))
        & (field(to, 3, 1) == field(index, 3, 1))
        & (field(to, 2, 1) == field(index, 4, 1))
        & (field(to, 1, 1) == field(index, 1, 1))
    )
    return marked(same, 0.125)


def lane_map():
    index, to = grid_of(512, 256)
    y = field(index, 0, 8)
    return marked(
        ((y >> 2) == field(to, 0, 6))
        & (field(y, 1, 1) == field(to, 7, 1))
        & (field(index, 8, 1) == field(to, 6, 1))
    )


def spread_map():
    index, y = grid_of(256, 256)
    return marked(((y >> 2) == field(index, 0, 6)) & (field(y, 1, 1) == field(index, 7, 1)))


def repeat_map():
    to, index = grid_of(32, 16)
    return marked(
        (field(to, 4, 1) == field(index, 0, 1))
        & (field(to, 3, 1) == field(index, 2, 1))
        & (field(to, 1, 1) == field(index, 1, 1))
    )


def over_points(matrix):
    rows, columns = matrix.shape
    wide = columns * 8
    high, low = two_terms(matrix)
    index, to = grid_of(columns, 3 * wide)
    source = (to >> 3) - jnp.where(to >= wide, columns, 0) - jnp.where(to >= 2 * wide, columns, 0)
    same = index == source
    spread = product(high, marked(same & (to < 2 * wide))) + product(
        low, marked(same & (to >= 2 * wide))
    )
    to, index = grid_of(rows * 8, rows)
    tall = product(marked((to >> 3) == index), spread.astype(BF16))
    row, column = grid_of(rows * 8, 3 * wide)
    return jnp.where((row & 7) == (column & 7), tall, 0.0).astype(BF16)


def column_of(row):
    tall = jnp.broadcast_to(row.astype(F32), (LANES, row.shape[1]))
    return jnp.transpose(tall).astype(jnp.int32)


def prepare_kernel(
    owner,
    schmid,
    latent,
    places,
    mailbox_row,
    tensor_map,
    harden_map,
    active_map,
    rows,
    lanes,
    repeat,
    spread,
    table,
):
    table[...] = jnp.broadcast_to(places[...], table.shape)
    owners = jnp.concatenate(
        [owner[i, j : j + 1] for i in range(owner.shape[0]) for j in range(owner.shape[1])],
        axis=1,
    )
    items = owners.shape[1]
    device = lax.broadcasted_iota(jnp.int32, (128, items), 0)
    onehot = (device == owners).astype(F32)
    index, to = grid_of(items, items)
    before = product(onehot.astype(BF16), marked(index < to))
    rank = jnp.sum(before * onehot, axis=0, keepdims=True).astype(jnp.int32)
    mailbox = owners * 8 + rank
    mailbox_row[...] = mailbox
    tensor_map[...] = over_points(schmid[...])
    harden_map[...] = over_points(latent[...])
    to, index = grid_of(active_map.shape[0], active_map.shape[1])
    active_map[...] = marked((to >> 3) == index)
    rows[...] = row_map()
    lanes[...] = lane_map()
    repeat[...] = repeat_map()
    spread[...] = spread_map()


def restrict_kernel(grains, rows, lanes, weights):
    orders, size_x, _, _ = grains.shape
    lefts = ([], [])
    for pair in range(orders // 2):
        parts = []
        for order in (2 * pair, 2 * pair + 1):
            for coarse in range(size_x // 2):
                low = grains[order, 2 * coarse]
                high = grains[order, 2 * coarse + 1]
                parts.append(low * low + high * high)
        summed = jnp.concatenate(parts, axis=0)
        moved = product(rows[...], jnp.concatenate(two_terms(summed), axis=0))
        for left, part in zip(lefts, two_terms(moved)):
            left.append(jnp.concatenate([part[:64], part[64:]], axis=1))
    found = product(jnp.concatenate(lefts[0], axis=0), lanes[...])
    found = found + product(jnp.concatenate(lefts[1], axis=0), lanes[...])
    row = lax.broadcasted_iota(jnp.int32, (found.shape[0], LANES), 0)
    picked = jnp.where(row % 2 == 0, found[:, :LANES], found[:, LANES:])
    for order in range(orders):
        for tile in range(4):
            start = (order * 4 + tile) * 8
            weights[order * 8 : order * 8 + 8, tile * LANES : (tile + 1) * LANES] = picked[
                start : start + 8
            ]


def prolonged(stored, repeat, spread, energy):
    high, low = two_terms(stored)
    rows = product(repeat, jnp.concatenate([high, low], axis=0))
    row = lax.broadcasted_iota(jnp.int32, rows.shape, 0)
    lane = lax.broadcasted_iota(jnp.int32, rows.shape, 1)
    rows = jnp.where((row // 4) % 2 == (lane // 64) % 2, rows, 0.0)
    tiles = [
        jnp.concatenate(
            [rows[:16, t * LANES : (t + 1) * LANES], rows[16:, t * LANES : (t + 1) * LANES]],
            axis=1,
        )
        for t in range(4)
    ]
    high, low = two_terms(jnp.concatenate(tiles, axis=0))
    cells = product(high, spread) + product(low, spread)
    for bx in range(2):
        for pair in range(2):
            for qx in range(2):
                start = ((bx * 2 + pair) * 2 + qx) * 8
                energy[bx * 2 + qx, pair * 8 : pair * 8 + 8] = cells[start : start + 8]


def mechanics_kernel(
    weights,
    strain,
    stress,
    resist,
    active,
    tensor_map,
    harden_map,
    active_map,
    repeat,
    spread,
    stress_out,
    resist_out,
    energy,
    tensor,
    rates,
    amounts,
):
    systems = active.shape[0]
    points = resist.shape[0] // systems
    items = weights.shape[1]
    high, low = two_terms(weights[...])
    tensor[...] = product(tensor_map[...], jnp.concatenate([high, low, high], axis=0))
    rates[...] = product(active_map[...], active[...].astype(BF16)) * SLIP_RATE

    def tile_step(tile, carry):
        lanes = pl.ds(pl.multiple_of(tile * WIDE, WIDE), WIDE)
        trial = [
            stress[points * c : points * (c + 1), lanes]
            + 2.0 * strain[points * c : points * (c + 1), lanes]
            for c in range(6)
        ]

        def sweep(_, now):
            sums = [jnp.zeros((points, WIDE), F32) for _ in range(6)]
            for a in range(systems):
                rows = pl.ds(a * points, points)
                parts = [tensor[pl.ds((a * 6 + c) * points, points), lanes] for c in range(6)]
                resolved = (
                    (parts[0] * now[0] + parts[1] * now[1])
                    + (parts[2] * now[2] + parts[3] * now[3])
                    + (parts[4] * now[4] + parts[5] * now[5])
                )
                slip = rates[rows, lanes] * resolved / (resist[rows, lanes] + jnp.abs(resolved))
                amounts[rows, lanes] = jnp.abs(slip)
                sums = [sums[c] + parts[c] * slip for c in range(6)]
            return tuple(trial[c] - 2.0 * sums[c] for c in range(6))

        now = lax.fori_loop(0, ITERS, sweep, tuple(trial))
        for c in range(6):
            stress_out[points * c : points * (c + 1), lanes] = now[c]
        return carry

    lax.fori_loop(0, items // WIDE, tile_step, 0)
    amount = amounts[...]
    high, low = two_terms(amount)
    harden = product(harden_map[...], jnp.concatenate([high, low, high], axis=0))
    grown = resist[...] + HARDENING * harden
    resist_out[...] = grown
    work = grown * amount
    stored = work[:points]
    for a in range(1, systems):
        stored = stored + work[points * a : points * (a + 1)]
    prolonged(stored, repeat[...], spread[...], energy)


def own_and_other(odd, even_value, odd_value):
    return jnp.where(odd > 0.0, odd_value, even_value)


def odd_x_of(table):
    return table[16:17]


def odd_z_of(table):
    return table[17:18]


def z_rows(table, order, x, z_pair, z_other):
    odd_z = odd_z_of(table)
    mate, other = z_pair[order, x : x + 1], z_other[order, x : x + 1]
    return own_and_other(odd_z, other, mate), own_and_other(odd_z, mate, other)


def new_layer(grains, x, lower, upper, z_pair, z_other, energy, table):
    orders, _, size_z, size_y = grains.shape
    row = lax.broadcasted_iota(jnp.int32, (size_z, size_y), 0)
    center = [grains[order, x] for order in range(orders)]
    squares = [value * value for value in center]
    total = squares[0]
    for order in range(1, orders):
        total = total + squares[order]
    shared = 2.0 * CROSS_TERM * total + 5.0
    cell = energy[x // 2]
    found = []
    for order in range(orders):
        value = center[order]
        first, last = 0.0, 0.0
        if z_pair is not None:
            first, last = z_rows(table, order, x, z_pair, z_other)
        below = jnp.where(row == 0, first, pltpu.roll(value, 1, 0))
        above = jnp.where(row == size_z - 1, last, pltpu.roll(value, size_z - 1, 0))
        around = (
            (lower(order) + upper(order))
            + (below + above)
            + (pltpu.roll(value, 1, 1) + pltpu.roll(value, size_y - 1, 1))
        )
        factor = shared + table[8 + order : 9 + order] * cell - 2.0 * squares[order]
        found.append(value + table[order : order + 1] * (around - value * factor))
    return found


def first_mechanics_kernel(*refs):
    count = 5
    sources, refs = refs[:count], refs[count:]
    inputs, refs = refs[:10], refs[10:]
    outputs, refs = refs[:3], refs[3:]
    targets, refs = refs[:count], refs[count:]
    scratch, sems = refs[:-1], refs[-1]
    copies = [
        pltpu.make_async_copy(source, target, sems.at[k])
        for k, (source, target) in enumerate(zip(sources, targets))
    ]
    for copy in copies:
        copy.start()
    mechanics_kernel(*inputs, *outputs, *scratch)
    for copy in copies:
        copy.wait()


def new_ends(grains, x_pair, x_other, odd_x, *others):
    last = grains.shape[1] - 1
    low = new_layer(
        grains,
        0,
        lambda order: own_and_other(odd_x, x_other[order], x_pair[order]),
        lambda order: grains[order, 1],
        *others,
    )
    high = new_layer(
        grains,
        last,
        lambda order: grains[order, last - 1],
        lambda order: own_and_other(odd_x, x_pair[order], x_other[order]),
        *others,
    )
    return low, high


def new_inner(grains, x, *others):
    return new_layer(
        grains,
        x,
        lambda order: grains[order, x - 1],
        lambda order: grains[order, x + 1],
        *others,
    )


def send_layers(odd_x, order, low, high, x_pair, x_other):
    x_pair[order] = own_and_other(odd_x, high, low)
    x_other[order] = own_and_other(odd_x, low, high)


def send_rows(odd_z, order, x, new, z_pair, z_other):
    size_z = new.shape[0]
    first, last = new[:1], new[size_z - 1 :]
    z_pair[order, x : x + 1] = own_and_other(odd_z, last, first)
    z_other[order, x : x + 1] = own_and_other(odd_z, first, last)


def edges_kernel(grains, table, x_pair, x_other, z_pair, z_other):
    orders, size_x, _, _ = grains.shape
    for order in range(orders):
        send_layers(
            odd_x_of(table), order, grains[order, 0], grains[order, size_x - 1], x_pair, x_other
        )
        for x in range(size_x):
            send_rows(odd_z_of(table), order, x, grains[order, x], z_pair, z_other)


def ends_kernel(
    grains,
    x_pair,
    x_other,
    z_pair,
    z_other,
    energy,
    table,
    x_pair_out,
    x_other_out,
):
    low, high = new_ends(
        grains, x_pair, x_other, odd_x_of(table), z_pair, z_other, energy, table
    )
    for order in range(grains.shape[0]):
        send_layers(odd_x_of(table), order, low[order], high[order], x_pair_out, x_other_out)


def first_inner_kernel(
    grains,
    z_pair,
    z_other,
    energy,
    x_pair_new,
    x_other_new,
    table,
    out,
    z_pair_out,
    z_other_out,
):
    orders, size_x, _, _ = grains.shape
    for order in range(orders):
        low = own_and_other(odd_x_of(table), x_other_new[order], x_pair_new[order])
        high = own_and_other(odd_x_of(table), x_pair_new[order], x_other_new[order])
        for x, new in ((0, low), (size_x - 1, high)):
            out[order, x] = new
            send_rows(odd_z_of(table), order, x, new, z_pair_out, z_other_out)
    for x in range(1, size_x - 1):
        found = new_inner(grains, x, z_pair, z_other, energy, table)
        for order in range(orders):
            out[order, x] = found[order]
            send_rows(odd_z_of(table), order, x, found[order], z_pair_out, z_other_out)


def second_inner_kernel(grains, energy, table, out):
    orders, size_x, _, _ = grains.shape
    for x in range(1, size_x - 1):
        found = new_inner(grains, x, None, None, energy, table)
        for order in range(orders):
            out[order, x] = found[order]


def end_rows(inner, order, x, z_pair, z_other, table):
    size_z = inner.shape[2]
    first, last = z_rows(table, order, x, z_pair, z_other)
    step = table[order : order + 1]
    return (
        inner[order, x, :1] + step * first,
        inner[order, x, size_z - 1 :] + step * last,
    )


def second_rows_kernel(
    inner, x_pair_new, x_other_new, z_pair, z_other, table, out, z_pair_out, z_other_out
):
    orders, size_x, size_z, _ = inner.shape
    odd_x, odd_z = odd_x_of(table), odd_z_of(table)
    for order in range(orders):
        low = own_and_other(odd_x, x_other_new[order], x_pair_new[order])
        high = own_and_other(odd_x, x_pair_new[order], x_other_new[order])
        for x, new in ((0, low), (size_x - 1, high)):
            out[order, x] = new
            send_rows(odd_z, order, x, new, z_pair_out, z_other_out)
        for x in range(1, size_x - 1):
            first, last = end_rows(inner, order, x, z_pair, z_other, table)
            out[order, x, :1] = first
            out[order, x, size_z - 1 :] = last
            z_pair_out[order, x : x + 1] = own_and_other(odd_z, last, first)
            z_other_out[order, x : x + 1] = own_and_other(odd_z, first, last)


def last_rows_kernel(inner, z_pair, z_other, table, out, held, sem):
    orders, size_x, size_z, _ = inner.shape
    for order in range(orders):
        for x in range(1, size_x - 1):
            first, last = end_rows(inner, order, x, z_pair, z_other, table)
            held[order, x] = inner[order, x]
            held[order, x, :1] = first
            held[order, x, size_z - 1 :] = last
    inside = (slice(None), slice(1, size_x - 1))
    copy = pltpu.make_async_copy(held.at[inside], out.at[inside], sem)
    copy.start()
    copy.wait()


def finish_kernel(
    grains,
    x_pair,
    x_other,
    z_pair,
    z_other,
    energy,
    table,
    inside,
    anchor,
    mail,
    out,
    stress,
    resist,
    held,
    sems,
):
    size_x = grains.shape[1]
    ends = new_ends(grains, x_pair, x_other, odd_x_of(table), z_pair, z_other, energy, table)
    copies = []
    for side, x in ((0, 0), (1, size_x - 1)):
        for order in range(grains.shape[0]):
            held[side, order] = ends[side][order]
        copies.append(pltpu.make_async_copy(held.at[side], out.at[:, x], sems.at[side]))
        copies[-1].start()
    unpack_result_kernel(anchor, mail, stress, resist)
    for copy in copies:
        copy.wait()


def swapped(value, axis, first):
    size = lax.axis_size(axis)
    pairs = [(i % size, (i + 1) % size) for i in range(first, size + first, 2)]
    return lax.ppermute(value, axis, pairs + [(j, i) for i, j in pairs])


def halos(edges):
    found = {}
    for place, axis, first in ((1, "gx", 1), (0, "gx", 0), (3, "gz", 1), (2, "gz", 0)):
        found[place] = swapped(edges[place], axis, first)
    return tuple(found[place] for place in range(4))


def shards(
    grains,
    block_owner,
    element_anchor,
    strain_step,
    stress,
    resistance,
    slip_active,
    orientation_schmid,
    latent_hardening,
    mobility,
    grain_state,
):
    count_all = lax.axis_size(("gx", "gz"))
    per_dev = element_anchor.shape[0]
    slots_all = 2 * per_dev
    orders, size_x, size_z, size_y = grains.shape
    points = stress.shape[1]
    systems = resistance.shape[0]
    tensors, forces = 6 * points, systems * points
    narrow = -(-(tensors + forces) // LANES) * LANES
    whole = pl.BlockSpec(memory_space=pltpu.VMEM)
    far = pl.BlockSpec(memory_space=pltpu.HBM)
    anchor = element_anchor.reshape(1, per_dev)
    message = 5 * slots_all // 2

    outbox = call(
        pack_state_kernel,
        shape(message, LANES),
        limit=None,
        scratch=(
            pltpu.VMEM((2 * tensors + forces, per_dev), F32),
            pltpu.VMEM((systems, per_dev), jnp.int32),
            pltpu.VMEM((slots_all, 2 * LANES), F32),
            pltpu.VMEM((slots_all, LANES), F32),
            pltpu.VMEM((message, LANES), F32),
            pltpu.SemaphoreType.DMA((4 + CHUNKS,)),
        ),
        in_specs=[whole, far, far, far, far],
        out_specs=far,
    )(
        anchor,
        strain_step.reshape(tensors, per_dev),
        stress.reshape(tensors, per_dev),
        resistance.reshape(forces, per_dev),
        slip_active,
    )
    inbox = exchanged(outbox.reshape(count_all, 5, 4, LANES)).reshape(message, LANES)

    places = jnp.concatenate(
        [
            TIME_STEP * mobility,
            2.0 * DRIVE_SCALE * (1.0 - grain_state),
            jnp.stack([lax.axis_index(name) % 2 for name in ("gx", "gz")]).astype(F32),
            jnp.zeros((6,), F32),
        ]
    ).reshape(24, 1)
    whole_number = functools.partial(jax.ShapeDtypeStruct, dtype=jnp.int32)
    half_wide = functools.partial(jax.ShapeDtypeStruct, dtype=BF16)
    (
        mailbox_row,
        tensor_map,
        harden_map,
        active_map,
        rows,
        lanes,
        repeat,
        spread,
        table,
    ) = call(
        prepare_kernel,
        (
            whole_number((1, per_dev)),
            half_wide((6 * forces, 3 * orders * points)),
            half_wide((forces, 3 * forces)),
            half_wide((forces, systems)),
            half_wide((128, 256)),
            half_wide((512, 256)),
            half_wide((32, 16)),
            half_wide((256, 256)),
            shape(24, size_y),
        ),
        limit=12,
    )(
        block_owner,
        orientation_schmid.reshape(orders, systems * 6).T,
        latent_hardening,
        places,
    )
    edge_shapes = (
        shape(orders, size_z, size_y),
        shape(orders, size_z, size_y),
        shape(orders, size_x, size_y),
        shape(orders, size_x, size_y),
    )
    edges = call(edges_kernel, edge_shapes, limit=4, in_specs=[whole] * 2)(grains, table)
    strain_h = stress_h = resist_h = active_h = None
    for cycle in range(STEPS):
        around = halos(edges)
        weights = call(restrict_kernel, shape(orders * points, per_dev), limit=8)(
            grains, rows, lanes
        )
        if cycle == 0:
            strain_h, stress_h, resist_h, active_h = call(
                unpack_state_kernel,
                (
                    shape(tensors, per_dev),
                    shape(tensors, per_dev),
                    shape(forces, per_dev),
                    shape(systems, per_dev),
                ),
                limit=16,
                in_specs=[far, whole],
                scratch=(
                    pltpu.VMEM((slots_all, 2 * LANES), F32),
                    pltpu.VMEM((slots_all // 2, LANES), F32),
                    pltpu.VMEM((1, per_dev), jnp.int32),
                    pltpu.SemaphoreType.DMA,
                ),
            )(mailbox_row, inbox)
        inputs = (
            weights,
            strain_h,
            stress_h,
            resist_h,
            active_h,
            tensor_map,
            harden_map,
            active_map,
            repeat,
            spread,
        )
        outputs = (
            shape(tensors, per_dev),
            shape(forces, per_dev),
            shape(size_x // 2, size_z, size_y),
        )
        scratch = (
            pltpu.VMEM((6 * forces, per_dev), F32),
            pltpu.VMEM((forces, per_dev), F32),
            pltpu.VMEM((forces, per_dev), F32),
        )
        if cycle == 0:
            stress_h, resist_h, energy, grains, *around = call(
                first_mechanics_kernel,
                outputs + (shape(orders, size_x, size_z, size_y),) + edge_shapes,
                limit=12,
                in_specs=[far] * 5 + [whole] * 10,
                out_specs=[whole] * 8,
                scratch=scratch + (pltpu.SemaphoreType.DMA((5,)),),
            )(grains, *around, *inputs)
        else:
            stress_h, resist_h, energy = call(
                mechanics_kernel, outputs, limit=12, scratch=scratch
            )(*inputs)
        if cycle == STEPS - 1:
            around, stress_h = lax.optimization_barrier((around, stress_h))
        around = tuple(around)
        brick = shape(orders, size_x, size_z, size_y)
        x_pair, x_other = call(
            ends_kernel, edge_shapes[:2], limit=4, in_specs=[whole] * 7
        )(grains, *around, energy, table)
        grains, z_pair, z_other = call(
            first_inner_kernel,
            (brick,) + edge_shapes[2:],
            limit=4,
            in_specs=[whole] * 7,
        )(grains, *around[2:], energy, x_pair, x_other, table)
        around = halos((x_pair, x_other, z_pair, z_other))
        inner = call(
            second_inner_kernel,
            brick,
            limit=4,
            in_specs=[whole] * 3,
            out_specs=whole,
        )(grains, energy, table)
        if cycle < STEPS - 1:
            x_pair, x_other = call(
                ends_kernel, edge_shapes[:2], limit=4, in_specs=[whole] * 7
            )(grains, *around, energy, table)
            grains, z_pair, z_other = call(
                second_rows_kernel,
                (brick,) + edge_shapes[2:],
                limit=4,
                in_specs=[whole] * 6,
                out_specs=[whole] * 3,
                input_output_aliases={0: 0},
            )(inner, x_pair, x_other, *around[2:], table)
            edges = (x_pair, x_other, z_pair, z_other)
    outbox = call(
        pack_result_kernel,
        shape(slots_all, narrow),
        limit=12,
        out_specs=far,
        scratch=(pltpu.VMEM((slots_all, narrow), F32), pltpu.SemaphoreType.DMA((CHUNKS,))),
    )(
        mailbox_row, stress_h, resist_h
    )
    inbox = exchanged(outbox.reshape(count_all, slots_all // count_all, narrow))
    inside = call(
        last_rows_kernel,
        brick,
        limit=4,
        in_specs=[whole] * 4,
        out_specs=far,
        scratch=(
            pltpu.VMEM((orders, size_x, size_z, size_y), F32),
            pltpu.SemaphoreType.DMA,
        ),
    )(inner, *around[2:], table)
    grains, stress, resistance = call(
        finish_kernel,
        (brick, shape(tensors, per_dev), shape(forces, per_dev)),
        limit=12,
        in_specs=[whole] * 7 + [far] + [whole] * 2,
        out_specs=[far, whole, whole],
        scratch=(
            pltpu.VMEM((2, orders, size_z, size_y), F32),
            pltpu.SemaphoreType.DMA((2,)),
        ),
        input_output_aliases={7: 0},
    )(grains, *around, energy, table, inside, anchor, inbox.reshape(slots_all, narrow))
    return (
        grains,
        stress.reshape(6, points, per_dev),
        resistance.reshape(systems, points, per_dev),
    )


def solution(mesh):
    return jax.shard_map(
        shards,
        mesh=mesh,
        in_specs=(
            P(None, "gx", "gz", None),
            P("gx", "gz", None),
            P(("gx", "gz")),
            P(None, None, ("gx", "gz")),
            P(None, None, ("gx", "gz")),
            P(None, None, ("gx", "gz")),
            P(None, ("gx", "gz")),
            P(),
            P(),
            P(),
            P(),
        ),
        out_specs=(
            P(None, "gx", "gz", None),
            P(None, None, ("gx", "gz")),
            P(None, None, ("gx", "gz")),
        ),
        check_vma=False,
    )
```
